32 devices in a mesh: pp: 2 (over core), fsdp: 4 (over y, x), tp: 4 (over z).
Axes of the slice: x: 2, y: 2, z: 4, core: 2. Of those that a mesh axis runs over, the one named last changes fastest.
Arguments:
- inputs: bfloat16 [2, 128, 8192], P(None, 'tp', 'fsdp'), may hold values from -12 to 12
- head_grad: bfloat16 [2, 128, 8192], P(None, 'tp', 'fsdp'), may hold values from -0.3 to 0.3
- noise_mask: int32 [2, 128], P(None, 'tp'), may hold values 0 or 1
- lengths: int32 [2, 4, 2], replicated, may hold values from 1 to 24, 32 in all within a row
- rewards: int32 [2, 4, 2], replicated, may hold values from 0 to 3
- groups: int32 [2, 4, 2], replicated, may hold values from 0 to 7, as said below
- query_weight: bfloat16 [2, 8192, 4096], P('pp', 'fsdp', 'tp'), may hold values from -0.0625 to 0.0625
- key_weight: bfloat16 [2, 8192, 1024], P('pp', 'fsdp', 'tp'), may hold values from -0.0625 to 0.0625
- value_weight: bfloat16 [2, 8192, 1024], P('pp', 'fsdp', 'tp'), may hold values from -1 to 1
- out_weight: bfloat16 [2, 4096, 8192], P('pp', 'tp', 'fsdp'), may hold values from -1 to 1
Outputs:
- query_weight_grad: float32 [2, 8192, 4096], P('pp', 'fsdp', 'tp')
- key_weight_grad: float32 [2, 8192, 1024], P('pp', 'fsdp', 'tp')
- value_weight_grad: float32 [2, 8192, 1024], P('pp', 'fsdp', 'tp')
- out_weight_grad: float32 [2, 4096, 8192], P('pp', 'tp', 'fsdp')
The draws below stay inside these ranges and needn't reach their ends.
Inputs may be any that keep to these rules, and one draw needn't show every extreme that they name: `groups`: every group value names exactly 2 completions.
All inputs are finite; a program needn't handle non-finite values. No bound on the sum of `noise_mask` on one device may be relied on, other than what follows from the above.
Results may differ from the reference program's by a relative error of at most 0.013.
Values may be sent and summed in bfloat16 or wider, within the bound.
No kernel may reach another device: no remote copies, remote signals or barrier semaphores. Data moves between devices by JAX's collectives and lax.ppermute only.
A program may use at most 128 MiB of HBM per device.

```python
import math
import jax
import jax.numpy as jnp
import numpy as np
from jax import lax

MODEL_WIDTH = 8192
KEY_VALUE_HEADS = 8
HEAD_WIDTH = 128
QUERY_HEADS = 32
SLOT = 32
MICRO = 2
CPS = 2
REWARD_TOP = 4
MOST = 24
TOKENS_MB = 128
HQD = 4096
HKD = 1024
N_PP = 2
N_FSDP = 4


def draw_groups(key, part):
    completions = MICRO * N_FSDP * CPS
    shuffled = jax.random.permutation(jax.random.fold_in(key, 7), completions)
    return (shuffled % (2 * N_FSDP)).reshape(MICRO, N_FSDP, CPS).astype(jnp.int32)


def stream_parts(key):
    row_total = SLOT * N_FSDP
    mixing = 0.6
    common = jax.random.normal(jax.random.fold_in(key, 11), (MICRO, 1, MODEL_WIDTH), jnp.float32)
    own = jax.random.normal(jax.random.fold_in(key, 12), (MICRO, row_total, MODEL_WIDTH), jnp.float32)
    token_scale = jnp.exp(jax.random.uniform(jax.random.fold_in(key, 13), (MICRO, row_total, 1), jnp.float32, -1.0, 1.0))
    unit = mixing * common + jnp.sqrt(1.0 - mixing * mixing) * own
    return (unit, token_scale)


def draw_inputs(key, part):
    feature = jnp.arange(MODEL_WIDTH, dtype=jnp.float32) / (MODEL_WIDTH - 1)
    unit, token_scale = stream_parts(key)
    scale_feature = 0.2 * jnp.exp(feature * jnp.log(10.0))
    return jnp.clip(unit * scale_feature * token_scale, -12.0, 12.0).astype(jnp.bfloat16)


def draw_head_grad(key, part):
    unit, token_scale = stream_parts(key)
    aligned = 0.8
    noise = jax.random.normal(jax.random.fold_in(key, 14), unit.shape, jnp.float32)
    value_list = 0.05 * (aligned * unit + jnp.sqrt(1.0 - aligned * aligned) * noise)
    return jnp.clip(value_list, -0.3, 0.3).astype(jnp.bfloat16)


def value_parts(key):
    value_list = jax.random.normal(jax.random.fold_in(key, 21), (N_PP, MODEL_WIDTH, KEY_VALUE_HEADS * HEAD_WIDTH), jnp.float32)
    return jnp.clip(value_list, -5.0, 5.0) * MODEL_WIDTH ** (-0.5)


def draw_value_weight(key, part):
    return value_parts(key).astype(jnp.bfloat16)


def draw_out_weight(key, part):
    value_gathered = value_parts(key)
    flipped_order = jnp.transpose(value_gathered, (0, 2, 1)).reshape(N_PP, KEY_VALUE_HEADS, 1, HEAD_WIDTH, MODEL_WIDTH)
    copied_state = jnp.broadcast_to(flipped_order, (N_PP, KEY_VALUE_HEADS, QUERY_HEADS // KEY_VALUE_HEADS, HEAD_WIDTH, MODEL_WIDTH)).reshape(N_PP, QUERY_HEADS * HEAD_WIDTH, MODEL_WIDTH)
    noise = jnp.clip(jax.random.normal(jax.random.fold_in(key, 22), (N_PP, QUERY_HEADS * HEAD_WIDTH, MODEL_WIDTH), jnp.float32), -5.0, 5.0)
    value_list = 0.75 ** 0.5 * (MODEL_WIDTH / (QUERY_HEADS * HEAD_WIDTH)) ** 0.5 * copied_state + 0.5 * noise * (QUERY_HEADS * HEAD_WIDTH) ** (-0.5)
    return value_list.astype(jnp.bfloat16)


def plant(array, key, low, largest):
    dims = array.shape
    index_at = [jax.random.randint(jax.random.fold_in(key, axis), (), 0, dims[axis]) for axis in range(len(dims))]
    array = array.at[tuple(index_at)].set(low)
    longest = dims.index(max(dims))
    index_at[longest] = (index_at[longest] + 1) % dims[longest]
    return array.at[tuple(index_at)].set(largest)


def levels(rng, extent, pieces, least, top_value):
    def one(axis_at, parts):
        draws = jax.random.uniform(jax.random.fold_in(jax.random.fold_in(rng, 6), axis_at), (parts,), jnp.float32, least / len(pieces), top_value / len(pieces))
        return jnp.repeat(jnp.exp(draws), extent[axis_at] // parts).reshape((-1,) + (1,) * (len(extent) - axis_at - 1))

    gain = one(*pieces[0])
    for cut in pieces[1:]:
        gain = gain * one(*cut)
    return gain


def length_profile(amount, total, most, skew):
    portions = [(1 << 20) // math.isqrt(standing ** skew) + 1 for standing in range(2, amount + 1)]
    rest, given = total - most - (amount - 1), [1] * (amount - 1)
    while rest > 0:
        movable = [i for i in range(amount - 1) if given[i] < most]
        whole, left = sum([portions[i] for i in movable]), rest
        for i in movable:
            addition = min(most - given[i], max(1, left * portions[i] // whole), rest)
            given[i] = given[i] + addition
            rest = rest - addition
    return np.array([most] + given)


def uneven_parts(stream_key, count, total, bound, slope):
    if count == 2:
        one = jax.random.randint(stream_key, (), max(1, total - bound), min(bound, total - 1) + 1)
        return jnp.stack([one, total - one])
    sizes = jnp.asarray(length_profile(count, total, bound, slope), jnp.int32)
    twos = (count - 1) // 2
    donor, receiver = sizes[1:1 + 2 * twos:2], sizes[2:2 + 2 * twos:2]
    margin = jnp.minimum(donor - 1, bound - receiver)
    passed = jax.random.randint(jax.random.fold_in(stream_key, 1), (twos,), 0, 1 << 20) % (margin + 1)
    sizes = sizes.at[1:1 + 2 * twos:2].set(donor - passed).at[2:2 + 2 * twos:2].set(receiver + passed)
    return sizes[jax.random.permutation(jax.random.fold_in(stream_key, 2), count)]


def gaussian(own_key, dims, spread, limit, pieces=(), held_as=jnp.bfloat16):
    drawn = jax.random.normal(own_key, dims, jnp.float32) * spread
    if len(pieces) > 0:
        drawn = levels(own_key, dims, pieces, -0.22, 0.18) * drawn
    return jnp.clip(drawn, min=-limit, max=limit).astype(held_as)


def setup_inputs(seed: int = 0) -> dict:
    key_list = jax.random.split(jax.random.key(seed), 11)
    inputs = draw_inputs(jax.random.fold_in(key_list[10], 71), 0)
    head_grad = draw_head_grad(jax.random.fold_in(key_list[10], 71), 0)
    noise_mask = plant((jax.random.randint(key_list[2], (MICRO, TOKENS_MB), 0, 2) < 1).astype(jnp.int32), jax.random.fold_in(key_list[2], 1), 0, 1)
    lengths = jax.vmap(lambda own: uneven_parts(own, CPS, SLOT, MOST, 2))(jax.random.split(key_list[3], MICRO * N_FSDP)).reshape((MICRO, N_FSDP, CPS)).astype(jnp.int32)
    rewards = plant(jax.random.randint(key_list[4], (MICRO, N_FSDP, CPS), 0, REWARD_TOP), jax.random.fold_in(key_list[4], 1), 0, REWARD_TOP - 1).astype(jnp.int32)
    groups = draw_groups(jax.random.fold_in(key_list[10], 71), 0)
    query_weight = gaussian(key_list[6], (N_PP, MODEL_WIDTH, HQD), MODEL_WIDTH ** -0.5, 0.0625, ((0, 2), (1, 4), (2, 4)))
    key_weight = gaussian(key_list[7], (N_PP, MODEL_WIDTH, HKD), MODEL_WIDTH ** -0.5, 0.0625, ((0, 2), (1, 4), (2, 4)))
    value_weight = draw_value_weight(jax.random.fold_in(key_list[10], 71), 0)
    out_weight = draw_out_weight(jax.random.fold_in(key_list[10], 71), 0)
    return dict(inputs=inputs, head_grad=head_grad, noise_mask=noise_mask, lengths=lengths, rewards=rewards, groups=groups, query_weight=query_weight, key_weight=key_weight, value_weight=value_weight, out_weight=out_weight)


epsilon = 1e-06
masked_score = -1e+30

def segments(lengths):
    segment_ends = jnp.cumsum(lengths, -1)
    position = jnp.arange(SLOT, dtype=jnp.int32)
    return lax.optimization_barrier(jnp.sum((segment_ends[..., None, :] <= position[:, None]).astype(jnp.int32), -1)).astype(jnp.int32)

def token_weights(lengths, rewards, groups):
    group_total = 2 * lengths.shape[1]
    reward_flat = rewards.reshape(-1).astype(jnp.float32)
    member = (groups.reshape(-1)[:, None] == jnp.arange(group_total, dtype=jnp.int32)[None, :]).astype(jnp.float32)
    member_count = lax.optimization_barrier(jnp.sum(member, 0))
    group_mean = lax.optimization_barrier(jnp.sum(member * reward_flat[:, None], 0)) / member_count
    centered = reward_flat - lax.optimization_barrier(jnp.sum(member * group_mean[None, :], 1))
    variance = lax.optimization_barrier(jnp.sum(member * (centered * centered)[:, None], 0)) / member_count
    spread_own = lax.optimization_barrier(jnp.sum(member * jnp.sqrt(variance)[None, :], 1))
    advantage = (centered / jnp.maximum(spread_own, 1.0)).reshape(lengths.shape)
    segment = segments(lengths)
    choose = (segment[..., None] == jnp.arange(lengths.shape[2], dtype=jnp.int32)).astype(jnp.float32)
    token_adv = lax.optimization_barrier(jnp.sum(choose * advantage[:, :, None, :], -1))
    token_len = lax.optimization_barrier(jnp.sum(choose * lengths[:, :, None, :].astype(jnp.float32), -1))
    return (token_adv * SLOT / token_len).reshape(lengths.shape[0], -1)

def split_heads(query_rows, key_rows, value_rows):
    batch_count, slot_len = (query_rows.shape[0], query_rows.shape[1])
    kv_heads = key_rows.shape[-1] // HEAD_WIDTH
    group_heads = query_rows.shape[-1] // HEAD_WIDTH // kv_heads
    query_heads = query_rows.reshape(batch_count, slot_len, kv_heads, group_heads, HEAD_WIDTH).astype(jnp.float32)
    key_heads = key_rows.reshape(batch_count, slot_len, kv_heads, HEAD_WIDTH).astype(jnp.float32)
    value_heads = value_rows.reshape(batch_count, slot_len, kv_heads, HEAD_WIDTH).astype(jnp.float32)
    return (query_heads, key_heads, value_heads)

def attend(query_rows, key_rows, value_rows, segment):
    query_heads, key_heads, value_heads = split_heads(query_rows, key_rows, value_rows)
    score_scale = HEAD_WIDTH ** (-0.5)
    scores = jnp.einsum('bikgd,bjkd->bkgij', query_heads, key_heads) * score_scale
    same_doc = segment[:, None, None, :, None] == segment[:, None, None, None, :]
    scores = jnp.where(same_doc, scores, masked_score)
    attn_probs = jax.nn.softmax(scores, axis=-1)
    rounded = lax.optimization_barrier(attn_probs.astype(jnp.bfloat16)).astype(jnp.float32)
    mixture = jnp.einsum('bkgij,bjkd->bikgd', rounded, value_heads)
    return (mixture.reshape(query_rows.shape).astype(jnp.bfloat16), attn_probs)

def attend_back(query_rows, key_rows, value_rows, attn_probs, head_out_grad):
    query_heads, key_heads, value_heads = split_heads(query_rows, key_rows, value_rows)
    score_scale = HEAD_WIDTH ** (-0.5)
    grad_heads = head_out_grad.reshape(query_heads.shape).astype(jnp.float32)
    rounded = lax.optimization_barrier(attn_probs.astype(jnp.bfloat16)).astype(jnp.float32)
    prob_grad = jnp.einsum('bikgd,bjkd->bkgij', grad_heads, value_heads)
    value_grad = jnp.einsum('bkgij,bikgd->bjkd', rounded, grad_heads)
    score_grad = attn_probs * (prob_grad - lax.optimization_barrier(jnp.sum(prob_grad * attn_probs, -1, keepdims=True)))
    score_grad = lax.optimization_barrier(score_grad.astype(jnp.bfloat16)).astype(jnp.float32)
    query_grad = jnp.einsum('bkgij,bjkd->bikgd', score_grad, key_heads) * score_scale
    key_grad = jnp.einsum('bkgij,bikgd->bjkd', score_grad, query_heads) * score_scale
    return (query_grad.reshape(query_rows.shape).astype(jnp.bfloat16), key_grad.reshape(key_rows.shape).astype(jnp.bfloat16), value_grad.reshape(value_rows.shape).astype(jnp.bfloat16))

def layer_forward(stream, query_layer, key_layer, value_layer, out_layer, segment):
    slot_total = segment.shape[0]
    stream_float = stream.astype(jnp.float32)
    inv_rms = lax.rsqrt(lax.optimization_barrier(jnp.mean(stream_float * stream_float, -1)) + epsilon)
    normed = (stream_float * inv_rms[:, None]).astype(jnp.bfloat16)
    query_rows = jnp.dot(normed, query_layer, preferred_element_type=jnp.float32).astype(jnp.bfloat16)
    key_rows = jnp.dot(normed, key_layer, preferred_element_type=jnp.float32).astype(jnp.bfloat16)
    value_rows = jnp.dot(normed, value_layer, preferred_element_type=jnp.float32).astype(jnp.bfloat16)
    head_out, attn_probs = attend(query_rows.reshape(slot_total, SLOT, -1), key_rows.reshape(slot_total, SLOT, -1), value_rows.reshape(slot_total, SLOT, -1), segment)
    head_out = head_out.reshape(stream.shape[0], -1)
    summed = jnp.dot(head_out, out_layer, preferred_element_type=jnp.float32)
    return ((stream_float + summed).astype(jnp.bfloat16), (inv_rms, normed, query_rows, key_rows, value_rows, attn_probs, head_out))

def layer_backward(out_grad, stream, kept_state, query_layer, key_layer, value_layer, out_layer):
    inv_rms, normed, query_rows, key_rows, value_rows, attn_probs, head_out = kept_state
    slot_total = stream.shape[0] // SLOT
    out_weight_grad = jnp.dot(head_out.T, out_grad, preferred_element_type=jnp.float32)
    head_out_grad = jnp.dot(out_grad, out_layer.T, preferred_element_type=jnp.float32).astype(jnp.bfloat16)
    query_grad, key_grad, value_grad = attend_back(query_rows.reshape(slot_total, SLOT, -1), key_rows.reshape(slot_total, SLOT, -1), value_rows.reshape(slot_total, SLOT, -1), attn_probs, head_out_grad.reshape(slot_total, SLOT, -1))
    query_grad = query_grad.reshape(stream.shape[0], -1)
    key_grad = key_grad.reshape(stream.shape[0], -1)
    value_grad = value_grad.reshape(stream.shape[0], -1)
    query_weight_grad = jnp.dot(normed.T, query_grad, preferred_element_type=jnp.float32)
    key_weight_grad = jnp.dot(normed.T, key_grad, preferred_element_type=jnp.float32)
    value_weight_grad = jnp.dot(normed.T, value_grad, preferred_element_type=jnp.float32)
    normed_grad = jnp.dot(query_grad, query_layer.T, preferred_element_type=jnp.float32) + jnp.dot(key_grad, key_layer.T, preferred_element_type=jnp.float32) + jnp.dot(value_grad, value_layer.T, preferred_element_type=jnp.float32)
    stream_float = stream.astype(jnp.float32)
    grad_dot = lax.optimization_barrier(jnp.sum(normed_grad * stream_float, -1))
    input_grad = (out_grad.astype(jnp.float32) + inv_rms[:, None] * normed_grad - stream_float * (inv_rms ** 3 * grad_dot / MODEL_WIDTH)[:, None]).astype(jnp.bfloat16)
    return (input_grad, (query_weight_grad, key_weight_grad, value_weight_grad, out_weight_grad))

def reference(inputs, head_grad, noise_mask, lengths, rewards, groups, query_weight, key_weight, value_weight, out_weight):
    segment_all = segments(lengths)
    weight_all = token_weights(lengths, rewards, groups) * noise_mask.astype(jnp.float32)
    totals = [jnp.zeros(query_weight.shape, jnp.float32), jnp.zeros(key_weight.shape, jnp.float32), jnp.zeros(value_weight.shape, jnp.float32), jnp.zeros(out_weight.shape, jnp.float32)]
    for micro_index in range(MICRO):
        stream = inputs[micro_index]
        history = []
        for layer_index in range(N_PP):
            following, kept_state = layer_forward(stream, query_weight[layer_index], key_weight[layer_index], value_weight[layer_index], out_weight[layer_index], segment_all[micro_index])
            history.append((stream, kept_state))
            stream = following
        out_grad = (-weight_all[micro_index][:, None] * head_grad[micro_index].astype(jnp.float32)).astype(jnp.bfloat16)
        for layer_index in range(N_PP - 1, -1, -1):
            stream, kept_state = history[layer_index]
            out_grad, terms = layer_backward(out_grad, stream, kept_state, query_weight[layer_index], key_weight[layer_index], value_weight[layer_index], out_weight[layer_index])
            for which in range(4):
                totals[which] = totals[which].at[layer_index].add(terms[which])
    return (totals[0], totals[1], totals[2], totals[3])
```

```python
import functools

import jax
import jax.numpy as jnp
from jax import lax
from jax.experimental import pallas as pl
from jax.experimental.pallas import tpu as pltpu
from jax.sharding import PartitionSpec as P

MODEL_WIDTH = 8192
HEAD_WIDTH = 128
SLOT = 32
LANES = 128
BLOCK = 128

epsilon = 1e-06
masked_score = -1e30
bf16 = jnp.bfloat16
f32 = jnp.float32


def segments(lengths):
    segment_ends = jnp.cumsum(lengths, -1)
    position = jnp.arange(SLOT, dtype=jnp.int32)
    return jnp.sum((segment_ends[..., None, :] <= position[:, None]).astype(jnp.int32), -1)


def token_weights(lengths, rewards, groups, segment):
    group_total = 2 * lengths.shape[1]
    reward_flat = rewards.reshape(-1).astype(f32)
    member = (
        groups.reshape(-1)[:, None] == jnp.arange(group_total, dtype=jnp.int32)[None, :]
    ).astype(f32)
    member_count = jnp.sum(member, 0)
    group_mean = jnp.sum(member * reward_flat[:, None], 0) / member_count
    centered = reward_flat - jnp.sum(member * group_mean[None, :], 1)
    variance = jnp.sum(member * (centered * centered)[:, None], 0) / member_count
    spread_own = jnp.sum(member * jnp.sqrt(variance)[None, :], 1)
    advantage = (centered / jnp.maximum(spread_own, 1.0)).reshape(lengths.shape)
    choose = (segment[..., None] == jnp.arange(lengths.shape[2], dtype=jnp.int32)).astype(f32)
    token_adv = jnp.sum(choose * advantage[:, :, None, :], -1)
    token_len = jnp.sum(choose * lengths[:, :, None, :].astype(f32), -1)
    return (token_adv * SLOT / token_len).reshape(lengths.shape[0], -1)


def exchange(value, axis, bit):
    count = lax.axis_size(axis)
    return lax.ppermute(value, axis, [(source, source ^ bit) for source in range(count)])


def call(body, outs, args, smem=(), hbm=(), scratch=(), flops=0):
    def spec(place):
        space = pltpu.SMEM if place in smem else pl.ANY if place in hbm else pltpu.VMEM
        return pl.BlockSpec(memory_space=space)

    moved = sum(a.size * a.dtype.itemsize for a in args) + sum(
        o.size * o.dtype.itemsize for o in outs
    )
    result = pl.pallas_call(
        body,
        out_shape=list(outs),
        in_specs=[spec(place) for place in range(len(args))],
        out_specs=[pl.BlockSpec(memory_space=pltpu.VMEM)] * len(outs),
        scratch_shapes=list(scratch),
        cost_estimate=pl.CostEstimate(flops=flops, bytes_accessed=moved, transcendentals=0),
    )(*args)
    return result


def shape(rows, columns, kind):
    return jax.ShapeDtypeStruct((rows, columns), kind)


def lane_of(rows):
    return lax.broadcasted_iota(jnp.int32, (rows, LANES), 1)


def first_lane(total):
    return jnp.where(lane_of(total.shape[0]) == 0, total, 0.0)


def high_low(total):
    high = total.astype(bf16).astype(f32)
    lane = lane_of(total.shape[0])
    return jnp.where(lane == 0, high, jnp.where(lane == 1, total - high, 0.0)).astype(bf16)


def fetch(core, layer, own, other, target, sem):
    rows = target.shape[0]
    mine = own.at[pl.ds(pl.multiple_of(core * rows, rows), rows), :]

    @pl.when(core == layer)
    def _():
        pltpu.make_async_copy(mine, target, sem).start()

    @pl.when(core != layer)
    def _():
        pltpu.make_async_copy(other, target, sem).start()

    return pltpu.make_async_copy(other, target, sem)


def part(index, size):
    return pl.ds(pl.multiple_of(index * size, LANES), size)


def project_kernel(
    layer, core_ref, x_ref, qo, ko, vo, qr, kr, vr, keep, send, wq, wk, wv, sems
):
    core = core_ref[0]
    waits = [
        fetch(core, layer, own, other, target, sems.at[place])
        for place, (own, other, target) in enumerate(((qo, qr, wq), (ko, kr, wk), (vo, vr, wv)))
    ]
    x = x_ref[...]
    wide = x.astype(f32)
    squares = jnp.sum(wide * wide, -1, keepdims=True)
    start = 0
    for weight, wait in zip((wq, wk, wv), waits):
        wait.wait()
        half = weight.shape[1] // 2
        keep[:, start : start + half] = jnp.dot(
            x, weight[:, part(core, half)], preferred_element_type=f32
        )
        send[:, start : start + half] = jnp.dot(
            x, weight[:, part(1 - core, half)], preferred_element_type=f32
        ).astype(bf16)
        start += half
    keep[:, start:] = first_lane(squares)
    send[:, start:] = high_low(squares)


def add_kernel(tail, counts, keep, *refs):
    recvs, out, sends = refs[: counts[0]], refs[counts[0]], refs[counts[0] + 1 :]
    columns = keep.shape[1] - (LANES if tail else 0)
    rows = keep.shape[0] // len(recvs)
    for place, recv in enumerate(recvs):
        span = slice(place * rows, (place + 1) * rows)
        out[span, :columns] = keep[span, :columns] + recv[:, :columns].astype(f32)
        if tail:
            total = jnp.sum(
                keep[span, columns:] + recv[:, columns:].astype(f32), -1, keepdims=True
            )
            out[span, columns:] = first_lane(total)
    if sends:
        rows = keep.shape[0] // len(sends)
        for place, send in enumerate(sends):
            span = slice(place * rows, (place + 1) * rows)
            send[:, :columns] = out[span, :columns].astype(bf16)
            if tail:
                send[:, columns:] = high_low(jnp.sum(out[span, columns:], -1, keepdims=True))


def add(keep, recvs, sends, tail):
    rows, columns = keep.shape
    outs = [shape(rows, columns, f32)] + [shape(rows // sends, columns, bf16)] * sends
    body = functools.partial(add_kernel, tail, (len(recvs), sends))
    return call(body, outs, [keep, *recvs])


def sum_fsdp(keep, sends, tail):
    bits = [1 << place for place in range(lax.axis_size("fsdp").bit_length() - 1)]
    middle = len(bits) // 2
    orders = (bits, bits[middle:] + bits[:middle])
    for place in range(len(bits)):
        recvs = [exchange(send, "fsdp", order[place]) for send, order in zip(sends, orders)]
        if place + 1 < len(bits):
            keep, *sends = add(keep, recvs, 2, tail)
    return keep, recvs


def attend(rows_ref, seg_col, seg_row, block, head, kv_place, group):
    span = slice(block * BLOCK, (block + 1) * BLOCK)
    heads_q = rows_ref.shape[1] // HEAD_WIDTH * group // (group + 2)
    kv_heads = heads_q // group
    query = rows_ref[span, head * HEAD_WIDTH : (head + 1) * HEAD_WIDTH]
    key_at = (heads_q + kv_place) * HEAD_WIDTH
    value_at = key_at + kv_heads * HEAD_WIDTH
    key = rows_ref[span, key_at : key_at + HEAD_WIDTH]
    value = rows_ref[span, value_at : value_at + HEAD_WIDTH]
    scores = lax.dot_general(
        query, key, (((1,), (1,)), ((), ())), preferred_element_type=f32
    ) * HEAD_WIDTH ** (-0.5)
    same = seg_col[span, :] == seg_row[0:1, span]
    scores = jnp.where(same, scores, masked_score)
    powers = jnp.exp(scores - jnp.max(scores, -1, keepdims=True))
    probs = powers / jnp.sum(powers, -1, keepdims=True)
    return span, query, key, value, probs


def attend_back(span, query, key, value, probs, rounded, grad):
    scale = HEAD_WIDTH ** (-0.5)
    prob_grad = lax.dot_general(
        grad, value, (((1,), (1,)), ((), ())), preferred_element_type=f32
    )
    value_grad = lax.dot_general(
        rounded, grad, (((0,), (0,)), ((), ())), preferred_element_type=f32
    )
    score_grad = probs * (prob_grad - jnp.sum(prob_grad * probs, -1, keepdims=True))
    score_grad = score_grad.astype(bf16)
    query_grad = jnp.dot(score_grad, key, preferred_element_type=f32) * scale
    key_grad = (
        lax.dot_general(score_grad, query, (((0,), (0,)), ((), ())), preferred_element_type=f32)
        * scale
    )
    return query_grad, key_grad, value_grad


def totals(keep, recvs, columns, span_rows):
    rows = keep.shape[0] // len(recvs)
    for place, recv in enumerate(recvs):
        yield slice(place * rows, (place + 1) * rows), recv


def make_rows(keep, recvs, rows_out, inv_out, raw):
    columns = rows_out.shape[1]
    height = keep.shape[0] // len(recvs)
    for place, recv in enumerate(recvs):
        span = slice(place * height, (place + 1) * height)
        total = keep[span, :columns] + recv[:, :columns].astype(f32)
        squares = jnp.sum(keep[span, columns:] + recv[:, columns:].astype(f32), -1, keepdims=True)
        inv_rms = lax.rsqrt(squares / MODEL_WIDTH + epsilon)
        inv_out[span, :] = jnp.broadcast_to(inv_rms, (height, LANES))
        rows_out[span, :] = (total * inv_rms).astype(bf16)
        if raw is not None:
            raw[span, :] = total


def forward_kernel(group, keep, recv_a, recv_b, seg_col, seg_row, rows_out, inv_out, heads_out):
    make_rows(keep, (recv_a, recv_b), rows_out, inv_out, None)
    heads = heads_out.shape[1] // HEAD_WIDTH
    for block in range(keep.shape[0] // BLOCK):
        for head in range(heads):
            span, _, _, value, probs = attend(
                rows_out, seg_col, seg_row, block, head, head // group, group
            )
            heads_out[span, head * HEAD_WIDTH : (head + 1) * HEAD_WIDTH] = jnp.dot(
                probs.astype(bf16), value, preferred_element_type=f32
            ).astype(bf16)


def back_blocks(group, rows_ref, seg_col, seg_row, grad_of, grads_out, heads_out):
    heads = rows_ref.shape[1] // HEAD_WIDTH * group // (group + 2)
    kv_heads = heads // group
    for block in range(rows_ref.shape[0] // BLOCK):
        for kv_place in range(kv_heads):
            key_sum = value_sum = None
            for head in range(kv_place * group, (kv_place + 1) * group):
                span, query, key, value, probs = attend(
                    rows_ref, seg_col, seg_row, block, head, kv_place, group
                )
                rounded = probs.astype(bf16)
                here = slice(head * HEAD_WIDTH, (head + 1) * HEAD_WIDTH)
                if heads_out is not None:
                    heads_out[span, here] = jnp.dot(
                        rounded, value, preferred_element_type=f32
                    ).astype(bf16)
                query_grad, key_grad, value_grad = attend_back(
                    span, query, key, value, probs, rounded, grad_of(span, here)
                )
                grads_out[span, here] = query_grad.astype(bf16)
                key_sum = key_grad if key_sum is None else key_sum + key_grad
                value_sum = value_grad if value_sum is None else value_sum + value_grad
            at = (heads + kv_place) * HEAD_WIDTH
            grads_out[span, at : at + HEAD_WIDTH] = key_sum.astype(bf16)
            at = at + kv_heads * HEAD_WIDTH
            grads_out[span, at : at + HEAD_WIDTH] = value_sum.astype(bf16)


def sum_grad(keep, recvs, target):
    height = keep.shape[0] // len(recvs)
    for place, recv in enumerate(recvs):
        span = slice(place * height, (place + 1) * height)
        target[span, :] = (keep[span, :] + recv[...].astype(f32)).astype(bf16)


def both_kernel(
    group, keep, recv_a, recv_b, grad_keep, grad_a, grad_b, seg_col, seg_row,
    inv_out, heads_out, grads_out, dots_out, rows, raw, grad,
):
    make_rows(keep, (recv_a, recv_b), rows, inv_out, raw)
    sum_grad(grad_keep, (grad_a, grad_b), grad)
    columns = rows.shape[1]
    back_blocks(
        group, rows, seg_col, seg_row, lambda span, here: grad[span, here], grads_out, heads_out
    )
    dots = jnp.sum(grads_out[:, :columns].astype(f32) * raw[...], -1, keepdims=True)
    dots_out[...] = first_lane(dots)
    grads_out[:, columns:] = high_low(dots)


def back_kernel(group, rows, grad_keep, grad_a, grad_b, seg_col, seg_row, grads_out, grad):
    sum_grad(grad_keep, (grad_a, grad_b), grad)
    back_blocks(
        group, rows, seg_col, seg_row, lambda span, here: grad[span, here], grads_out, None
    )


def out_kernel(layer, core_ref, heads, own, other, keep, send, weight, sem):
    core = core_ref[0]
    fetch(core, layer, own, other, weight, sem).wait()
    half = weight.shape[1] // 2
    keep[...] = jnp.dot(heads[...], weight[:, part(core, half)], preferred_element_type=f32)
    send[...] = jnp.dot(
        heads[...], weight[:, part(1 - core, half)], preferred_element_type=f32
    ).astype(bf16)


def halve_kernel(keep, recv, out, send):
    half = keep.shape[0] // 2
    out[...] = keep[:half, :] + recv[:half, :].astype(f32)
    send[...] = (keep[half:, :] + recv[half:, :].astype(f32)).astype(bf16)


def stream_kernel(keep, recv, stream, out):
    quarter = keep.shape[0] // 2
    for place in range(2):
        span = slice(place * quarter, (place + 1) * quarter)
        back = slice((1 - place) * quarter, (2 - place) * quarter)
        total = keep[span, :] + recv[back, :].astype(f32)
        out[span, :] = (stream[span, :].astype(f32) + total).astype(bf16)


def grad_kernel(keep, recv, grad, stream, inv_ref, out):
    quarter = keep.shape[0] // 2
    columns = out.shape[1]
    for place in range(2):
        span = slice(place * quarter, (place + 1) * quarter)
        back = slice((1 - place) * quarter, (2 - place) * quarter)
        total = keep[span, :columns] + recv[back, :columns].astype(f32)
        dots = jnp.sum(keep[span, columns:] + recv[back, columns:].astype(f32), -1, keepdims=True)
        inv_rms = inv_ref[span, 0:1]
        out[span, :] = (
            grad[span, :].astype(f32)
            + inv_rms * total
            - stream[span, :].astype(f32) * (inv_rms * inv_rms * inv_rms * dots / MODEL_WIDTH)
        ).astype(bf16)


def heads_kernel(layer, core_ref, own_grad, other_grad, own, other, keep, *rest):
    sends, (weight, sem) = rest[:-2], rest[-2:]
    core = core_ref[0]
    fetch(core, layer, own, other, weight, sem).wait()
    half = weight.shape[1] // 2
    turned = (((1,), (1,)), ((), ()))
    keep[...] = lax.dot_general(
        own_grad[...], weight[:, part(core, half)], turned, preferred_element_type=f32
    ) + lax.dot_general(
        other_grad[...], weight[:, part(1 - core, half)], turned, preferred_element_type=f32
    )
    rows = keep.shape[0] // len(sends)
    for place, send in enumerate(sends):
        send[...] = keep[place * rows : (place + 1) * rows, :].astype(bf16)


def normed_kernel(
    layer, core_ref, own_grads, other_grads, dots, qo, ko, vo, qr, kr, vr,
    keep, send, wq, wk, wv, total, sems,
):
    core = core_ref[0]
    waits = [
        fetch(core, layer, own, other, target, sems.at[place])
        for place, (own, other, target) in enumerate(((qo, qr, wq), (ko, kr, wk), (vo, vr, wv)))
    ]
    turned = (((1,), (1,)), ((), ()))
    start = 0
    for weight, wait in zip((wq, wk, wv), waits):
        wait.wait()
        half = weight.shape[1] // 2
        term = lax.dot_general(
            own_grads[:, start : start + half], weight[:, part(core, half)], turned,
            preferred_element_type=f32,
        ) + lax.dot_general(
            other_grads[:, start : start + half], weight[:, part(1 - core, half)], turned,
            preferred_element_type=f32,
        )
        total[...] = term if start == 0 else total[...] + term
        start += half
    half = total.shape[0] // 2
    columns = total.shape[1]
    dot_total = jnp.sum(dots[...] + other_grads[:, start:].astype(f32), -1, keepdims=True)
    keep[:, :columns] = total[:half, :]
    keep[:, columns:] = first_lane(dot_total[:half])
    send[:, :columns] = total[half:, :].astype(bf16)
    send[:, columns:] = high_low(dot_total[half:])


def gather_tokens(own):
    near, far, cross = (exchange(own, "tp", bit) for bit in (1, 2, 3))
    return jnp.concatenate([own, far, near, cross])


def local(
    inputs, head_grad, noise_mask, lengths, rewards, groups,
    query_weight, key_weight, value_weight, out_weight,
):
    core = lax.axis_index("pp")
    shard = lax.axis_index("tp")
    micro, own_rows, features = inputs.shape
    half = features // 2
    piece = micro * own_rows
    rows = 4 * piece
    own = [query_weight[0], key_weight[0], value_weight[0], out_weight[0]]
    group = own[0].shape[1] // own[1].shape[1]
    head_cols = own[0].shape[1] // 2
    kv_cols = own[1].shape[1] // 2
    columns = head_cols + 2 * kv_cols
    core_vec = core.astype(jnp.int32)[None]

    own_inputs = lax.dynamic_slice_in_dim(inputs, core * half, half, 2).reshape(piece, half)
    stream0 = gather_tokens(own_inputs)

    def swap(value):
        return exchange(value, "pp", 1)

    other = [
        swap(lax.dynamic_slice_in_dim(w, (1 - core) * (w.shape[0] // 2), w.shape[0] // 2, 0))
        for w in own
    ]

    segment = segments(lengths)
    weight_all = token_weights(lengths, rewards, groups, segment)
    own_weights = lax.dynamic_slice_in_dim(
        weight_all, shard * own_rows, own_rows, 1
    ) * noise_mask.astype(f32)
    own_head = lax.dynamic_slice_in_dim(head_grad, core * half, half, 2)
    top_grad = (-own_weights[:, :, None] * own_head.astype(f32)).astype(bf16).reshape(piece, half)

    slots = segment.shape[1]
    named = segment + lengths.shape[2] * (
        jnp.arange(micro, dtype=jnp.int32)[:, None, None] * slots
        + jnp.arange(slots, dtype=jnp.int32)[None, :, None]
    )
    named = jnp.swapaxes(named.reshape(micro, 4, own_rows), 0, 1).reshape(4, piece)
    order = shard ^ jnp.array([0, 2, 1, 3], jnp.int32)
    pick = (order[:, None] == jnp.arange(4, dtype=jnp.int32)[None, :]).astype(jnp.int32)
    named = jnp.sum(pick[:, :, None] * named[None], 1).reshape(rows)
    seg_col = jnp.broadcast_to(named[:, None], (rows, LANES))
    seg_row = jnp.broadcast_to(named[None, :], (8, rows))

    def project(layer, stream):
        depth, cols = half, columns + LANES
        args = [core_vec, stream, *own[:3], *other[:3]]
        keep, send = call(
            functools.partial(project_kernel, layer),
            [shape(rows, cols, f32), shape(rows, cols, bf16)],
            args,
            smem=(0,),
            hbm=range(2, 8),
            scratch=[pltpu.VMEM((depth, w.shape[1]), bf16) for w in own[:3]]
            + [pltpu.SemaphoreType.DMA((3,))],
            flops=4 * rows * half * columns,
        )
        keep, *sends = add(keep, [swap(send)], 2, True)
        return sum_fsdp(keep, sends, True)

    def head_grads(layer, grad, grad_other):
        keep, *sends = call(
            functools.partial(heads_kernel, layer),
            [shape(rows, head_cols, f32)] + [shape(rows // 2, head_cols, bf16)] * 2,
            [core_vec, grad, grad_other, own[3], other[3]],
            smem=(0,),
            hbm=(3, 4),
            scratch=[pltpu.VMEM((head_cols, features), bf16), pltpu.SemaphoreType.DMA],
            flops=2 * rows * features * head_cols,
        )
        return keep, sends

    keep, (recv_a, recv_b) = project(0, stream0)
    rows0, inv0, heads0 = call(
        functools.partial(forward_kernel, group),
        [shape(rows, columns, bf16), shape(rows, LANES, f32), shape(rows, head_cols, bf16)],
        [keep, recv_a, recv_b, seg_col, seg_row],
        flops=4 * rows * BLOCK * head_cols,
    )

    top_grad, stream0 = lax.optimization_barrier((top_grad, stream0))
    grad1 = gather_tokens(top_grad)
    grad1_other = swap(grad1)
    head_keep, head_sends = head_grads(1, grad1, grad1_other)
    heads0, head_sends = lax.optimization_barrier((heads0, head_sends))

    keep, send = call(
        functools.partial(out_kernel, 0),
        [shape(rows, half, f32), shape(rows, half, bf16)],
        [core_vec, heads0, own[3], other[3]],
        smem=(0,),
        hbm=(2, 3),
        scratch=[pltpu.VMEM((head_cols, features), bf16), pltpu.SemaphoreType.DMA],
        flops=2 * rows * features * head_cols,
    )
    keep, send = call(
        halve_kernel, [shape(rows // 2, half, f32), shape(rows // 2, half, bf16)], [keep, swap(send)]
    )
    keep, send = add(keep, [exchange(send, "tp", 1)], 1, False)
    (stream1,) = call(
        stream_kernel,
        [shape(rows // 2, half, bf16)],
        [keep, exchange(send, "tp", 2), stream0[: rows // 2]],
    )
    stream1 = jnp.concatenate([stream1, exchange(stream1, "tp", 1)])
    head_keep, (head_a, head_b) = sum_fsdp(head_keep, head_sends, False)

    keep, (recv_a, recv_b) = project(1, stream1)
    inv1, heads1, grads1, dots = call(
        functools.partial(both_kernel, group),
        [
            shape(rows, LANES, f32),
            shape(rows, head_cols, bf16),
            shape(rows, columns + LANES, bf16),
            shape(rows, LANES, f32),
        ],
        [keep, recv_a, recv_b, head_keep, head_a, head_b, seg_col, seg_row],
        scratch=[
            pltpu.VMEM((rows, columns), bf16),
            pltpu.VMEM((rows, columns), f32),
            pltpu.VMEM((rows, head_cols), bf16),
        ],
        flops=14 * rows * BLOCK * head_cols,
    )
    grads1_other = swap(grads1)
    keep, send = call(
        functools.partial(normed_kernel, 1),
        [shape(rows // 2, half + LANES, f32), shape(rows // 2, half + LANES, bf16)],
        [core_vec, grads1, grads1_other, dots, *own[:3], *other[:3]],
        smem=(0,),
        hbm=range(4, 10),
        scratch=[pltpu.VMEM((half, w.shape[1]), bf16) for w in own[:3]]
        + [pltpu.VMEM((rows, half), f32), pltpu.SemaphoreType.DMA((3,))],
        flops=4 * rows * half * columns,
    )
    keep, send = add(keep, [exchange(send, "tp", 1)], 1, True)
    (grad0,) = call(
        grad_kernel,
        [shape(rows // 2, half, bf16)],
        [
            keep,
            exchange(send, "tp", 2),
            grad1[: rows // 2],
            stream1[: rows // 2],
            inv1[: rows // 2],
        ],
    )
    grad0 = jnp.concatenate([grad0, exchange(grad0, "tp", 1)])

    grad0_other = swap(grad0)
    head_keep, head_sends = head_grads(0, grad0, grad0_other)
    head_keep, (head_a, head_b) = sum_fsdp(head_keep, head_sends, False)
    (grads0,) = call(
        functools.partial(back_kernel, group),
        [shape(rows, columns, bf16)],
        [rows0, head_keep, head_a, head_b, seg_col, seg_row],
        scratch=[pltpu.VMEM((rows, head_cols), bf16)],
        flops=12 * rows * BLOCK * head_cols,
    )

    first = core == 0
    inv = jnp.where(first, inv0[:, :1], inv1[:, :1])

    def ordered(mine, theirs):
        return jnp.concatenate(
            [jnp.where(first, mine, theirs), jnp.where(first, theirs, mine)], 1
        )

    stream_other = swap(jnp.where(first, stream1, stream0))
    stream_own = jnp.where(first, stream0, stream1)
    normed = (ordered(stream_own, stream_other).astype(f32) * inv).astype(bf16)
    heads_other = swap(jnp.where(first, heads1, heads0))
    heads_all = ordered(jnp.where(first, heads0, heads1), heads_other)
    grad_all = ordered(
        jnp.where(first, grad0, grad1), jnp.where(first, grad0_other, grad1_other)
    )
    grads0_other = swap(grads0)
    grads = jnp.where(first, grads0, grads1[:, :columns])
    grads_other = jnp.where(first, grads0_other, grads1_other[:, :columns])

    def weight_grad(left, right):
        return jnp.einsum("tm,tq->mq", left, right, preferred_element_type=f32)[None]

    cuts = (slice(0, head_cols), slice(head_cols, head_cols + kv_cols), slice(head_cols + kv_cols, columns))
    query_all, key_all, value_all = (ordered(grads[:, cut], grads_other[:, cut]) for cut in cuts)
    return (
        weight_grad(normed, query_all),
        weight_grad(normed, key_all),
        weight_grad(normed, value_all),
        weight_grad(heads_all, grad_all),
    )


def solution(mesh):
    return jax.shard_map(
        local,
        mesh=mesh,
        in_specs=(
            P(None, "tp", "fsdp"),
            P(None, "tp", "fsdp"),
            P(None, "tp"),
            P(),
            P(),
            P(),
            P("pp", "fsdp", "tp"),
            P("pp", "fsdp", "tp"),
            P("pp", "fsdp", "tp"),
            P("pp", "tp", "fsdp"),
        ),
        out_specs=(
            P("pp", "fsdp", "tp"),
            P("pp", "fsdp", "tp"),
            P("pp", "fsdp", "tp"),
            P("pp", "tp", "fsdp"),
        ),
        check_vma=False,
    )
```

```python
import functools
import math

import jax
import jax.numpy as jnp
from jax import lax
from jax.experimental import pallas as pl
from jax.experimental.pallas import tpu as pltpu
from jax.sharding import PartitionSpec as P


MODEL_WIDTH = 8192
HEAD_WIDTH = 128
SLOT = 32
LANES = 128
BLOCK = 128

epsilon = 1e-06
masked_score = -1e30

bf16 = jnp.bfloat16
f32 = jnp.float32


def exchange(value, axis, bit):
    count = lax.axis_size(axis)
    return lax.ppermute(value, axis, [(source, source ^ bit) for source in range(count)])


def call(body, outs, args, smem=(), hbm=(), scratch=(), flops=0):
    def spec(place):
        space = pltpu.SMEM if place in smem else pltpu.HBM if place in hbm else pltpu.VMEM
        return pl.BlockSpec(memory_space=space)

    def size(array):
        return math.prod(array.shape) * jnp.dtype(array.dtype).itemsize

    moved = sum(size(a) for a in args) + sum(size(o) for o in outs)
    held = sum(size(a) for place, a in enumerate(args) if place not in hbm)
    held += sum(size(o) for o in outs)
    held += sum(size(s) for s in scratch if hasattr(s, "memory_space") and s.memory_space == pltpu.VMEM)
    result = pl.pallas_call(
        body,
        out_shape=list(outs),
        in_specs=[spec(place) for place in range(len(args))],
        out_specs=[pl.BlockSpec(memory_space=pltpu.VMEM)] * len(outs),
        scratch_shapes=list(scratch),
        cost_estimate=pl.CostEstimate(flops=flops, bytes_accessed=moved, transcendentals=0),
        compiler_params=pltpu.CompilerParams(vmem_limit_bytes=held + (4 << 20)),
    )(*args)
    return result


def shape(rows, columns, kind):
    return jax.ShapeDtypeStruct((rows, columns), kind)


def lane_of(rows):
    return lax.broadcasted_iota(jnp.int32, (rows, LANES), 1)


def first_lane(total):
    return jnp.where(lane_of(total.shape[0]) == 0, total, 0.0)


def high_low(total):
    high = total.astype(bf16).astype(f32)
    lane = lane_of(total.shape[0])
    return jnp.where(lane == 0, high, jnp.where(lane == 1, total - high, 0.0)).astype(bf16)


def part(index, size):
    return pl.ds(pl.multiple_of(index * size, LANES), size)


def take(layer, core_ref, count, *refs):
    own, other, sems = refs[:count], refs[count : 2 * count], refs[-1]
    keep, send = refs[2 * count : 2 * count + 2]
    core = core_ref[0]
    rows = keep.shape[0]
    span = pl.ds(pl.multiple_of(core * rows, rows), rows)

    def copies(sources):
        start, found = 0, []
        for place, source in enumerate(sources):
            half = source.shape[1] // 2
            for side, target in enumerate((keep, send)):
                index = core if side == 0 else 1 - core
                found.append(
                    pltpu.make_async_copy(
                        source.at[span, part(index, half)],
                        target.at[:, start : start + half],
                        sems.at[2 * place + side],
                    )
                )
            start += half
        return found

    @pl.when(core == layer)
    def _():
        for copy in copies(own):
            copy.start()

    @pl.when(core != layer)
    def _():
        for copy in copies(other):
            copy.start()

    for copy in copies(other):
        copy.wait()


def project_kernel(x_ref, wkeep, wsend, keep, send):
    columns = wkeep.shape[1]
    x = x_ref[...]
    wide = x.astype(f32)
    squares = jnp.sum(wide * wide, -1, keepdims=True)
    send[:, :columns] = jnp.dot(x, wsend[...], preferred_element_type=f32).astype(bf16)
    send[:, columns:] = high_low(squares)
    keep[:, :columns] = jnp.dot(x, wkeep[...], preferred_element_type=f32)
    keep[:, columns:] = first_lane(squares)


def add_kernel(tail, counts, keep, *refs):
    recvs, out, sends = refs[: counts[0]], refs[counts[0]], refs[counts[0] + 1 :]
    columns = keep.shape[1] - (LANES if tail else 0)
    rows = keep.shape[0] // len(recvs)
    for place, recv in enumerate(recvs):
        span = slice(place * rows, (place + 1) * rows)
        out[span, :columns] = keep[span, :columns] + recv[:, :columns].astype(f32)
        if tail:
            total = jnp.sum(
                keep[span, columns:] + recv[:, columns:].astype(f32), -1, keepdims=True
            )
            out[span, columns:] = first_lane(total)
    if sends:
        rows = keep.shape[0] // len(sends)
        for place, send in enumerate(sends):
            span = slice(place * rows, (place + 1) * rows)
            send[:, :columns] = out[span, :columns].astype(bf16)
            if tail:
                send[:, columns:] = high_low(jnp.sum(out[span, columns:], -1, keepdims=True))


def add(keep, recvs, sends, tail):
    rows, columns = keep.shape
    outs = [shape(rows, columns, f32)] + [shape(rows // sends, columns, bf16)] * sends
    body = functools.partial(add_kernel, tail, (len(recvs), sends))
    return call(body, outs, [keep, *recvs])


def sum_fsdp(keep, sends, tail):
    bits = [1 << place for place in range(lax.axis_size("fsdp").bit_length() - 1)]
    middle = len(bits) // 2
    orders = (bits, bits[middle:] + bits[:middle])
    for place in range(len(bits)):
        recvs = [exchange(send, "fsdp", order[place]) for send, order in zip(sends, orders)]
        if place + 1 < len(bits):
            keep, *sends = add(keep, recvs, 2, tail)
    return keep, recvs


def stacked(ref, span, start, group):
    return jnp.concatenate(
        [ref[span, (start + g) * HEAD_WIDTH : (start + g + 1) * HEAD_WIDTH] for g in range(group)]
    )


def unstack(ref, span, start, group, value):
    for g in range(group):
        ref[span, (start + g) * HEAD_WIDTH : (start + g + 1) * HEAD_WIDTH] = value[
            g * BLOCK : (g + 1) * BLOCK
        ]


def attend(rows_ref, seg_col, seg_row, span, kv_place, kv_heads, group):
    heads = kv_heads * group
    query = stacked(rows_ref, span, kv_place * group, group)
    key = stacked(rows_ref, span, heads + kv_place, 1)
    value = stacked(rows_ref, span, heads + kv_heads + kv_place, 1)
    scores = lax.dot_general(
        query, key, (((1,), (1,)), ((), ())), preferred_element_type=f32
    ) * HEAD_WIDTH ** (-0.5)
    same = seg_col[span, :] == seg_row[0:1, span]
    scores = jnp.where(jnp.concatenate([same] * group), scores, masked_score)
    powers = jnp.exp(scores - jnp.max(scores, -1, keepdims=True))
    probs = powers / jnp.sum(powers, -1, keepdims=True)
    return query, key, value, probs


def attend_back(query, key, value, probs, rounded, grad):
    scale = HEAD_WIDTH ** (-0.5)
    prob_grad = lax.dot_general(
        grad, value, (((1,), (1,)), ((), ())), preferred_element_type=f32
    )
    value_grad = lax.dot_general(
        rounded, grad, (((0,), (0,)), ((), ())), preferred_element_type=f32
    )
    score_grad = probs * (prob_grad - jnp.sum(prob_grad * probs, -1, keepdims=True))
    score_grad = score_grad.astype(bf16)
    query_grad = jnp.dot(score_grad, key, preferred_element_type=f32) * scale
    key_grad = (
        lax.dot_general(score_grad, query, (((0,), (0,)), ((), ())), preferred_element_type=f32)
        * scale
    )
    return query_grad, key_grad, value_grad


def make_rows(keep, recvs, rows_out, inv_out, raw):
    columns = rows_out.shape[1]
    height = keep.shape[0] // len(recvs)
    for place, recv in enumerate(recvs):
        span = slice(place * height, (place + 1) * height)
        total = keep[span, :columns] + recv[:, :columns].astype(f32)
        squares = jnp.sum(keep[span, columns:] + recv[:, columns:].astype(f32), -1, keepdims=True)
        inv_rms = lax.rsqrt(squares / MODEL_WIDTH + epsilon)
        inv_out[span, :] = jnp.broadcast_to(inv_rms, (height, LANES))
        rows_out[span, :] = (total * inv_rms).astype(bf16)
        if raw is not None:
            raw[span, :] = total


def forward_kernel(group, keep, recv_a, recv_b, seg_col, seg_row, rows_out, inv_out, heads_out):
    make_rows(keep, (recv_a, recv_b), rows_out, inv_out, None)
    kv_heads = heads_out.shape[1] // HEAD_WIDTH // group
    for block in range(keep.shape[0] // BLOCK):
        span = slice(block * BLOCK, (block + 1) * BLOCK)
        for kv_place in range(kv_heads):
            _, _, value, probs = attend(
                rows_out, seg_col, seg_row, span, kv_place, kv_heads, group
            )
            mixed = jnp.dot(probs.astype(bf16), value, preferred_element_type=f32)
            unstack(heads_out, span, kv_place * group, group, mixed.astype(bf16))


def back_blocks(group, rows_ref, seg_col, seg_row, grad_ref, grads_out, heads_out):
    kv_heads = rows_ref.shape[1] // HEAD_WIDTH // (group + 2)
    heads = kv_heads * group
    for block in range(rows_ref.shape[0] // BLOCK):
        span = slice(block * BLOCK, (block + 1) * BLOCK)
        for kv_place in range(kv_heads):
            query, key, value, probs = attend(
                rows_ref, seg_col, seg_row, span, kv_place, kv_heads, group
            )
            rounded = probs.astype(bf16)
            if heads_out is not None:
                mixed = jnp.dot(rounded, value, preferred_element_type=f32)
                unstack(heads_out, span, kv_place * group, group, mixed.astype(bf16))
            grad = stacked(grad_ref, span, kv_place * group, group)
            query_grad, key_grad, value_grad = attend_back(
                query, key, value, probs, rounded, grad
            )
            unstack(grads_out, span, kv_place * group, group, query_grad.astype(bf16))
            unstack(grads_out, span, heads + kv_place, 1, key_grad.astype(bf16))
            unstack(grads_out, span, heads + kv_heads + kv_place, 1, value_grad.astype(bf16))


def sum_grad(keep, recvs, target):
    height = keep.shape[0] // len(recvs)
    for place, recv in enumerate(recvs):
        span = slice(place * height, (place + 1) * height)
        target[span, :] = (keep[span, :] + recv[...].astype(f32)).astype(bf16)


def both_kernel(
    group, keep, recv_a, recv_b, grad_keep, grad_a, grad_b, seg_col, seg_row,
    inv_out, heads_out, grads_out, dots_out, rows, raw, grad,
):
    make_rows(keep, (recv_a, recv_b), rows, inv_out, raw)
    sum_grad(grad_keep, (grad_a, grad_b), grad)
    columns = rows.shape[1]
    back_blocks(group, rows, seg_col, seg_row, grad, grads_out, heads_out)
    dots = jnp.sum(grads_out[:, :columns].astype(f32) * raw[...], -1, keepdims=True)
    dots_out[...] = first_lane(dots)
    grads_out[:, columns:] = high_low(dots)


def back_kernel(group, rows, grad_keep, grad_a, grad_b, seg_col, seg_row, grads_out, grad):
    sum_grad(grad_keep, (grad_a, grad_b), grad)
    back_blocks(group, rows, seg_col, seg_row, grad, grads_out, None)


def out_kernel(heads, wkeep, wsend, keep, send):
    send[...] = jnp.dot(heads[...], wsend[...], preferred_element_type=f32).astype(bf16)
    keep[...] = jnp.dot(heads[...], wkeep[...], preferred_element_type=f32)


def halve_kernel(keep, recv, out, send):
    half = keep.shape[0] // 2
    out[...] = keep[:half, :] + recv[:half, :].astype(f32)
    send[...] = (keep[half:, :] + recv[half:, :].astype(f32)).astype(bf16)


def stream_kernel(keep, recv, stream, out):
    quarter = keep.shape[0] // 2
    for place in range(2):
        span = slice(place * quarter, (place + 1) * quarter)
        back = slice((1 - place) * quarter, (2 - place) * quarter)
        total = keep[span, :] + recv[back, :].astype(f32)
        out[span, :] = (stream[span, :].astype(f32) + total).astype(bf16)


def grad_kernel(keep, recv, grad, stream, inv_ref, out):
    quarter = keep.shape[0] // 2
    columns = out.shape[1]
    for place in range(2):
        span = slice(place * quarter, (place + 1) * quarter)
        back = slice((1 - place) * quarter, (2 - place) * quarter)
        total = keep[span, :columns] + recv[back, :columns].astype(f32)
        dots = jnp.sum(keep[span, columns:] + recv[back, columns:].astype(f32), -1, keepdims=True)
        inv_rms = inv_ref[span, 0:1]
        out[span, :] = (
            grad[span, :].astype(f32)
            + inv_rms * total
            - stream[span, :].astype(f32) * (inv_rms * inv_rms * inv_rms * dots / MODEL_WIDTH)
        ).astype(bf16)


turned = (((1,), (1,)), ((), ()))


def heads_kernel(own_grad, other_grad, wkeep, wsend, keep, *sends):
    keep[...] = lax.dot_general(
        own_grad[...], wkeep[...], turned, preferred_element_type=f32
    ) + lax.dot_general(other_grad[...], wsend[...], turned, preferred_element_type=f32)
    rows = keep.shape[0] // len(sends)
    for place, send in enumerate(sends):
        send[...] = keep[place * rows : (place + 1) * rows, :].astype(bf16)


def normed_kernel(own_grads, other_grads, dots, wkeep, wsend, keep, send, total):
    inner, columns = wkeep.shape[1], wkeep.shape[0]
    half = keep.shape[0]
    total[...] = lax.dot_general(
        own_grads[:, :inner], wkeep[...], turned, preferred_element_type=f32
    )
    total[...] += lax.dot_general(
        other_grads[:, :inner], wsend[...], turned, preferred_element_type=f32
    )
    dot_total = jnp.sum(dots[...] + other_grads[:, inner:].astype(f32), -1, keepdims=True)
    keep[:, :columns] = total[:half, :]
    keep[:, columns:] = first_lane(dot_total[:half])
    send[:, :columns] = total[half:, :].astype(bf16)
    send[:, columns:] = high_low(dot_total[half:])


def prelude_kernel(
    place_ref, lengths, rewards, groups, mask, head, grad_out, seg_col, seg_row
):
    core, shard = place_ref[0], place_ref[1]
    micro, slots, packed = lengths.shape
    own_slots = slots // 4
    half = grad_out.shape[1]

    def ends(m, slot):
        found, total = [], 0
        for c in range(packed):
            total = total + lengths[m, slot, c]
            found.append(total)
        return found

    def named(m, slot, position):
        name = jnp.full(position.shape, (m * slots + slot) * packed, jnp.int32)
        for end in ends(m, slot):
            name = name + (end <= position).astype(jnp.int32)
        return name

    down = lax.broadcasted_iota(jnp.int32, (SLOT, LANES), 0)
    across = lax.broadcasted_iota(jnp.int32, (8, BLOCK), 1)
    per_block = BLOCK // SLOT
    line = None
    for at in range(4 * micro * own_slots):
        position, m, s = at // (micro * own_slots), at // own_slots % micro, at % own_slots
        slot = (shard ^ (0, 2, 1, 3)[position]) * own_slots + s
        seg_col[at * SLOT : (at + 1) * SLOT, :] = named(m, slot, down)
        inside = at % per_block
        name = named(m, slot, across - inside * SLOT)
        line = name if inside == 0 else jnp.where(across >= inside * SLOT, name, line)
        if inside == per_block - 1:
            first = (at // per_block) * BLOCK
            seg_row[:, first : first + BLOCK] = line

    own_rows = own_slots * SLOT
    for m in range(micro):
        wide = mask[m : m + 1, :].astype(f32)
        turn = lax.broadcasted_iota(jnp.int32, (own_rows, own_rows), 0) == (
            lax.broadcasted_iota(jnp.int32, (own_rows, own_rows), 1)
        )
        masks = jnp.sum(
            jnp.where(turn, jnp.broadcast_to(wide, (own_rows, own_rows)), 0.0), -1, keepdims=True
        )
        for s in range(own_slots):
            slot = shard * own_slots + s
            position = lax.broadcasted_iota(jnp.int32, (SLOT, 1), 0)
            advantage = jnp.zeros((SLOT, 1), f32)
            length = jnp.ones((SLOT, 1), f32)
            before = 0
            for c, end in enumerate(ends(m, slot)):
                mine = groups[m, slot, c]

                def gather(index, carry):
                    total, count, squares = carry
                    other_m = index // (slots * packed)
                    other_s = index // packed % slots
                    other_c = index % packed
                    same = groups[other_m, other_s, other_c] == mine
                    reward = rewards[other_m, other_s, other_c]
                    return (
                        total + jnp.where(same, reward, 0),
                        count + jnp.where(same, 1, 0),
                        squares + jnp.where(same, reward * reward, 0),
                    )

                total, count, squares = lax.fori_loop(
                    0, micro * slots * packed, gather, (jnp.int32(0), jnp.int32(0), jnp.int32(0))
                )

                def column(value):
                    return jnp.full((SLOT, 1), value, jnp.int32).astype(f32)

                centered = column(count * rewards[m, slot, c] - total) / column(count)
                spread = jnp.sqrt(column(count * squares - total * total)) / column(count)
                value = centered / jnp.maximum(spread, 1.0)
                here = (position >= before) & (position < end)
                advantage = jnp.where(here, value, advantage)
                length = jnp.where(here, column(lengths[m, slot, c]), length)
                before = end
            span = slice(s * SLOT, (s + 1) * SLOT)
            weight = -(advantage * SLOT / length * masks[span])
            grad_out[m * own_rows + s * SLOT : m * own_rows + (s + 1) * SLOT, :] = (
                weight * head[m, span, part(core, half)].astype(f32)
            ).astype(bf16)


def turn_kernel(core_ref, one, two, inv_one, inv_two, other, scale_out):
    core = core_ref[0]
    half = one.shape[1]
    first = core == 0
    if inv_one is not None:
        inv = jnp.where(first, inv_one[...], inv_two[...])[:, 0:1]
    for index, value in ((core, None), (1 - core, other[...])):
        if value is None:
            value = jnp.where(first, one[...].astype(f32), two[...].astype(f32))
        value = value.astype(f32)
        if inv_one is not None:
            value = value * inv
        scale_out[part(index, half), :] = value.T.astype(bf16)


def turn_plain_kernel(core_ref, one, two, other, out):
    turn_kernel(core_ref, one, two, None, None, other, out)


def weights_kernel(core_ref, left, *refs):
    rights, outs = refs[:4], refs[4:]
    core = core_ref[0]
    first = core == 0
    start = 0
    for out in outs:
        half = out.shape[1] // 2
        for side in range(2):
            cut = slice(start, start + half)
            right = jnp.where(first, rights[side][:, cut], rights[2 + side][:, cut])
            index = core if side == 0 else 1 - core
            out[:, part(index, half)] = jnp.dot(left[...], right, preferred_element_type=f32)
        start += half


def weight_grads(core_vec, left, rights, widths):
    rows, inner = left.shape
    block = min(512, rows)
    outs = [jax.ShapeDtypeStruct((rows, width), f32) for width in widths]

    def whole(array):
        return pl.BlockSpec(array.shape, lambda i: (0, 0))

    return pl.pallas_call(
        weights_kernel,
        grid=(rows // block,),
        out_shape=outs,
        in_specs=[
            pl.BlockSpec(memory_space=pltpu.SMEM),
            pl.BlockSpec((block, inner), lambda i: (i, 0)),
            *[whole(right) for right in rights],
        ],
        out_specs=[pl.BlockSpec((block, width), lambda i: (i, 0)) for width in widths],
        cost_estimate=pl.CostEstimate(
            flops=2 * rows * inner * sum(widths),
            bytes_accessed=4 * rows * sum(widths),
            transcendentals=0,
        ),
        compiler_params=pltpu.CompilerParams(vmem_limit_bytes=20 << 20),
    )(core_vec, left, *rights)


def spread_tokens(own):
    near, far, cross = (exchange(own, "tp", bit) for bit in (1, 2, 3))
    return [own, far, near, cross]


def local(
    inputs, head_grad, noise_mask, lengths, rewards, groups,
    query_weight, key_weight, value_weight, out_weight,
):
    core = lax.axis_index("pp")
    shard = lax.axis_index("tp")
    micro, own_rows, features = inputs.shape
    half = features // 2
    piece = micro * own_rows
    rows = 4 * piece
    own = [query_weight[0], key_weight[0], value_weight[0], out_weight[0]]
    group = own[0].shape[1] // own[1].shape[1]
    head_cols = own[0].shape[1] // 2
    kv_cols = own[1].shape[1] // 2
    columns = head_cols + 2 * kv_cols
    core_vec = core.astype(jnp.int32)[None]
    place_vec = jnp.stack([core, shard]).astype(jnp.int32)

    def swap(value):
        return exchange(value, "pp", 1)

    def after(value, *others):
        return lax.optimization_barrier((value, *others))[0]

    own_inputs = lax.dynamic_slice_in_dim(inputs, core * half, half, 2).reshape(piece, half)
    pieces = spread_tokens(own_inputs)
    other = [swap(w) for w in own[:3]]
    top_grad, seg_col, seg_row = call(
        prelude_kernel,
        [
            shape(piece, half, bf16),
            shape(rows, LANES, jnp.int32),
            shape(8, rows, jnp.int32),
        ],
        [place_vec, lengths, rewards, groups, noise_mask, head_grad],
        smem=range(4),
    )

    def taken(layer, mine, theirs, height):
        width = sum(w.shape[1] for w in mine) // 2
        return call(
            lambda core_ref, *refs: take(layer, core_ref, len(mine), *refs),
            [shape(height, width, bf16)] * 2,
            [core_vec, *mine, *theirs],
            smem=(0,),
            hbm=range(1, 1 + 2 * len(mine)),
            scratch=[pltpu.SemaphoreType.DMA((2 * len(mine),))],
        )

    in_weights = [taken(0, own[:3], other, half)]
    in_weights.append(taken(1, own[:3], other, half))
    stream0 = jnp.concatenate(pieces)
    other_out = swap(after(own[3], stream0))
    out_weights = [taken(layer, own[3:], [other_out], head_cols) for layer in (0, 1)]

    def project(layer, stream):
        cols = columns + LANES
        keep, send = call(
            project_kernel,
            [shape(rows, cols, f32), shape(rows, cols, bf16)],
            [stream, *in_weights[layer]],
            flops=4 * rows * half * columns,
        )
        keep, *sends = add(keep, [swap(send)], 2, True)
        return sum_fsdp(keep, sends, True)

    def head_grads(layer, grad, grad_other):
        keep, *sends = call(
            heads_kernel,
            [shape(rows, head_cols, f32)] + [shape(rows // 2, head_cols, bf16)] * 2,
            [grad, grad_other, *out_weights[layer]],
            flops=2 * rows * features * head_cols,
        )
        return keep, sends

    top_pieces = spread_tokens(after(top_grad, stream0))
    keep, (recv_a, recv_b) = project(0, stream0)
    rows0, inv0, heads0 = call(
        functools.partial(forward_kernel, group),
        [shape(rows, columns, bf16), shape(rows, LANES, f32), shape(rows, head_cols, bf16)],
        [keep, recv_a, recv_b, seg_col, seg_row],
        flops=4 * rows * BLOCK * head_cols,
    )

    keep, send = call(
        out_kernel,
        [shape(rows, half, f32), shape(rows, half, bf16)],
        [heads0, *out_weights[0]],
        flops=2 * rows * features * head_cols,
    )
    keep, send = call(
        halve_kernel, [shape(rows // 2, half, f32), shape(rows // 2, half, bf16)], [keep, swap(send)]
    )
    recv = exchange(send, "tp", 1)
    grad1 = jnp.concatenate(after(top_pieces, send))
    grad1_other = swap(grad1)
    head_keep, head_sends = head_grads(1, grad1, grad1_other)
    recv, head_keep, head_sends = lax.optimization_barrier((recv, head_keep, head_sends))
    keep, send = add(keep, [recv], 1, False)
    recv = exchange(send, "tp", 2)
    bits = lax.axis_size("fsdp").bit_length() - 1
    head_recvs = None
    if bits == 2:
        head_recvs = [exchange(value, "fsdp", bit) for value, bit in zip(head_sends, (1, 2))]
        head_keep, *head_sends = add(head_keep, head_recvs, 2, False)
        recv, head_keep, head_sends = lax.optimization_barrier((recv, head_keep, head_sends))
    (stream1,) = call(
        stream_kernel, [shape(rows // 2, half, bf16)], [keep, recv, stream0[: rows // 2]]
    )
    recv = exchange(stream1, "tp", 1)
    if bits == 2:
        head_a, head_b = [exchange(value, "fsdp", bit) for value, bit in zip(head_sends, (2, 1))]
    else:
        head_keep, (head_a, head_b) = sum_fsdp(head_keep, head_sends, False)
    recv, head_a, head_b = lax.optimization_barrier((recv, head_a, head_b))
    stream1 = jnp.concatenate([stream1, recv])

    keep, (recv_a, recv_b) = project(1, stream1)
    inv1, heads1, grads1, dots = call(
        functools.partial(both_kernel, group),
        [
            shape(rows, LANES, f32),
            shape(rows, head_cols, bf16),
            shape(rows, columns + LANES, bf16),
            shape(rows, LANES, f32),
        ],
        [keep, recv_a, recv_b, head_keep, head_a, head_b, seg_col, seg_row],
        scratch=[
            pltpu.VMEM((rows, columns), bf16),
            pltpu.VMEM((rows, columns), f32),
            pltpu.VMEM((rows, head_cols), bf16),
        ],
        flops=14 * rows * BLOCK * head_cols,
    )
    grads1_other = swap(grads1)
    keep, send = call(
        normed_kernel,
        [shape(rows // 2, half + LANES, f32), shape(rows // 2, half + LANES, bf16)],
        [grads1, grads1_other, dots, *in_weights[1]],
        scratch=[pltpu.VMEM((rows, half), f32)],
        flops=4 * rows * half * columns,
    )
    recv = exchange(send, "tp", 1)

    first = core == 0
    stream0_late, stream1_late, heads0_late, heads1_late = lax.optimization_barrier(
        (stream0, stream1, heads0, heads1, send)
    )[:4]
    stream_other = swap(jnp.where(first, stream1_late, stream0_late))
    (normed,) = call(
        turn_kernel,
        [shape(features, rows, bf16)],
        [core_vec, stream0_late, stream1_late, inv0, inv1, stream_other],
        smem=(0,),
    )
    recv, normed = lax.optimization_barrier((recv, normed))
    keep, send = add(keep, [recv], 1, True)
    recv = exchange(send, "tp", 2)
    heads_other = swap(after(jnp.where(first, heads1_late, heads0_late), send))
    (heads_turned,) = call(
        turn_plain_kernel,
        [shape(2 * head_cols, rows, bf16)],
        [core_vec, heads0_late, heads1_late, heads_other],
        smem=(0,),
    )
    recv, heads_turned = lax.optimization_barrier((recv, heads_turned))
    (grad0,) = call(
        grad_kernel,
        [shape(rows // 2, half, bf16)],
        [keep, recv, grad1[: rows // 2], stream1[: rows // 2], inv1[: rows // 2]],
    )
    grad0 = jnp.concatenate([grad0, exchange(grad0, "tp", 1)])

    grad0_other = swap(grad0)
    head_keep, head_sends = head_grads(0, grad0, grad0_other)
    (out_weight_grad,) = weight_grads(
        core_vec, heads_turned, [grad0, grad0_other, grad1, grad1_other], [features]
    )
    head_keep, head_recvs = sum_fsdp(head_keep, head_sends, False)
    head_a, head_b, out_weight_grad = lax.optimization_barrier((*head_recvs, out_weight_grad))
    (grads0,) = call(
        functools.partial(back_kernel, group),
        [shape(rows, columns, bf16)],
        [rows0, head_keep, head_a, head_b, seg_col, seg_row],
        scratch=[pltpu.VMEM((rows, head_cols), bf16)],
        flops=12 * rows * BLOCK * head_cols,
    )
    in_grads = weight_grads(
        core_vec,
        normed,
        [grads0, swap(grads0), grads1, grads1_other],
        [2 * head_cols, 2 * kv_cols, 2 * kv_cols],
    )
    return tuple(grad[None] for grad in (*in_grads, out_weight_grad))


def solution(mesh):
    return jax.shard_map(
        local,
        mesh=mesh,
        in_specs=(
            P(None, "tp", "fsdp"),
            P(None, "tp", "fsdp"),
            P(None, "tp"),
            P(),
            P(),
            P(),
            P("pp", "fsdp", "tp"),
            P("pp", "fsdp", "tp"),
            P("pp", "fsdp", "tp"),
            P("pp", "tp", "fsdp"),
        ),
        out_specs=(
            P("pp", "fsdp", "tp"),
            P("pp", "fsdp", "tp"),
            P("pp", "fsdp", "tp"),
            P("pp", "tp", "fsdp"),
        ),
        check_vma=False,
    )
```

```python
import functools
import math

import jax
import jax.numpy as jnp
from jax import lax
from jax.experimental import pallas as pl
from jax.experimental.pallas import tpu as pltpu
from jax.sharding import PartitionSpec as P


MODEL_WIDTH = 8192
HEAD_WIDTH = 128
SLOT = 32
LANES = 128
BLOCK = 128

epsilon = 1e-06
masked_score = -1e30

bf16 = jnp.bfloat16
f32 = jnp.float32


def exchange(value, axis, bit):
    count = lax.axis_size(axis)
    return lax.ppermute(value, axis, [(source, source ^ bit) for source in range(count)])


def call(body, outs, args, smem=(), hbm=(), scratch=(), flops=0):
    def spec(place):
        space = pltpu.SMEM if place in smem else pltpu.HBM if place in hbm else pltpu.VMEM
        return pl.BlockSpec(memory_space=space)

    def size(array):
        return math.prod(array.shape) * jnp.dtype(array.dtype).itemsize

    moved = sum(size(a) for a in args) + sum(size(o) for o in outs)
    held = sum(size(a) for place, a in enumerate(args) if place not in hbm)
    held += sum(size(o) for o in outs)
    held += sum(size(s) for s in scratch if hasattr(s, "memory_space") and s.memory_space == pltpu.VMEM)
    result = pl.pallas_call(
        body,
        out_shape=list(outs),
        in_specs=[spec(place) for place in range(len(args))],
        out_specs=[pl.BlockSpec(memory_space=pltpu.VMEM)] * len(outs),
        scratch_shapes=list(scratch),
        cost_estimate=pl.CostEstimate(flops=flops, bytes_accessed=moved, transcendentals=0),
        compiler_params=pltpu.CompilerParams(vmem_limit_bytes=held + (4 << 20)),
    )(*args)
    return result


def shape(rows, columns, kind):
    return jax.ShapeDtypeStruct((rows, columns), kind)


def lane_of(rows):
    return lax.broadcasted_iota(jnp.int32, (rows, LANES), 1)


def first_lane(total):
    return jnp.where(lane_of(total.shape[0]) == 0, total, 0.0)


def high_low(total):
    high = total.astype(bf16).astype(f32)
    lane = lane_of(total.shape[0])
    return jnp.where(lane == 0, high, jnp.where(lane == 1, total - high, 0.0)).astype(bf16)


def part(index, size):
    return pl.ds(pl.multiple_of(index * size, LANES), size)


def take(layer, core_ref, count, *refs):
    own, other, sems = refs[:count], refs[count : 2 * count], refs[-1]
    keep, send = refs[2 * count : 2 * count + 2]
    core = core_ref[0]
    rows = keep.shape[0]
    span = pl.ds(pl.multiple_of(core * rows, rows), rows)

    def copies(sources):
        start, found = 0, []
        for place, source in enumerate(sources):
            half = source.shape[1] // 2
            for side, target in enumerate((keep, send)):
                index = core if side == 0 else 1 - core
                found.append(
                    pltpu.make_async_copy(
                        source.at[span, part(index, half)],
                        target.at[:, start : start + half],
                        sems.at[2 * place + side],
                    )
                )
            start += half
        return found

    @pl.when(core == layer)
    def _():
        for copy in copies(own):
            copy.start()

    @pl.when(core != layer)
    def _():
        for copy in copies(other):
            copy.start()

    for copy in copies(other):
        copy.wait()


def assemble(pieces, out):
    row = column = 0
    for piece in pieces:
        height, width = piece.shape
        out[row : row + height, column : column + width] = piece[...]
        column += width
        if column == out.shape[1]:
            row, column = row + height, 0


def join_kernel(*refs):
    assemble(refs[:-1], refs[-1])


def project_kernel(count, *refs):
    pieces, (wkeep, wsend, keep, send, x_out) = refs[:count], refs[count:]
    columns = wkeep.shape[1]
    assemble(pieces, x_out)
    x = x_out[...]
    wide = x.astype(f32)
    squares = jnp.sum(wide * wide, -1, keepdims=True)
    send[:, :columns] = jnp.dot(x, wsend[...], preferred_element_type=f32).astype(bf16)
    send[:, columns:] = high_low(squares)
    keep[:, :columns] = jnp.dot(x, wkeep[...], preferred_element_type=f32)
    keep[:, columns:] = first_lane(squares)


def add_kernel(tail, counts, keep, *refs):
    recvs, out, sends = refs[: counts[0]], refs[counts[0]], refs[counts[0] + 1 :]
    columns = keep.shape[1] - (LANES if tail else 0)
    rows = keep.shape[0] // len(recvs)
    for place, recv in enumerate(recvs):
        span = slice(place * rows, (place + 1) * rows)
        out[span, :columns] = keep[span, :columns] + recv[:, :columns].astype(f32)
        if tail:
            total = jnp.sum(
                keep[span, columns:] + recv[:, columns:].astype(f32), -1, keepdims=True
            )
            out[span, columns:] = first_lane(total)
    if sends:
        rows = keep.shape[0] // len(sends)
        for place, send in enumerate(sends):
            span = slice(place * rows, (place + 1) * rows)
            send[:, :columns] = out[span, :columns].astype(bf16)
            if tail:
                send[:, columns:] = high_low(jnp.sum(out[span, columns:], -1, keepdims=True))


def add(keep, recvs, sends, tail):
    rows, columns = keep.shape
    outs = [shape(rows, columns, f32)] + [shape(rows // sends, columns, bf16)] * sends
    body = functools.partial(add_kernel, tail, (len(recvs), sends))
    return call(body, outs, [keep, *recvs])


def sum_fsdp(keep, sends, tail):
    bits = [1 << place for place in range(lax.axis_size("fsdp").bit_length() - 1)]
    middle = len(bits) // 2
    orders = (bits, bits[middle:] + bits[:middle])
    for place in range(len(bits)):
        recvs = [exchange(send, "fsdp", order[place]) for send, order in zip(sends, orders)]
        if place + 1 < len(bits):
            keep, *sends = add(keep, recvs, 2, tail)
    return keep, recvs


def stacked(ref, span, start, group):
    return jnp.concatenate(
        [ref[span, (start + g) * HEAD_WIDTH : (start + g + 1) * HEAD_WIDTH] for g in range(group)]
    )


def unstack(ref, span, start, group, value):
    for g in range(group):
        ref[span, (start + g) * HEAD_WIDTH : (start + g + 1) * HEAD_WIDTH] = value[
            g * BLOCK : (g + 1) * BLOCK
        ]


def attend(rows_ref, seg_col, seg_row, span, kv_place, kv_heads, group):
    heads = kv_heads * group
    query = stacked(rows_ref, span, kv_place * group, group)
    key = stacked(rows_ref, span, heads + kv_place, 1)
    value = stacked(rows_ref, span, heads + kv_heads + kv_place, 1)
    scores = lax.dot_general(
        query, key, (((1,), (1,)), ((), ())), preferred_element_type=f32
    ) * HEAD_WIDTH ** (-0.5)
    same = seg_col[span, :] == seg_row[0:1, span]
    scores = jnp.where(jnp.concatenate([same] * group), scores, masked_score)
    powers = jnp.exp(scores - jnp.max(scores, -1, keepdims=True))
    probs = powers / jnp.sum(powers, -1, keepdims=True)
    return query, key, value, probs


def attend_back(query, key, value, probs, rounded, grad):
    scale = HEAD_WIDTH ** (-0.5)
    prob_grad = lax.dot_general(
        grad, value, (((1,), (1,)), ((), ())), preferred_element_type=f32
    )
    value_grad = lax.dot_general(
        rounded, grad, (((0,), (0,)), ((), ())), preferred_element_type=f32
    )
    score_grad = probs * (prob_grad - jnp.sum(prob_grad * probs, -1, keepdims=True))
    score_grad = score_grad.astype(bf16)
    query_grad = jnp.dot(score_grad, key, preferred_element_type=f32) * scale
    key_grad = (
        lax.dot_general(score_grad, query, (((0,), (0,)), ((), ())), preferred_element_type=f32)
        * scale
    )
    return query_grad, key_grad, value_grad


def make_rows(keep, recvs, rows_out, inv_out, raw):
    columns = rows_out.shape[1]
    height = keep.shape[0] // len(recvs)
    for place, recv in enumerate(recvs):
        span = slice(place * height, (place + 1) * height)
        total = keep[span, :columns] + recv[:, :columns].astype(f32)
        squares = jnp.sum(keep[span, columns:] + recv[:, columns:].astype(f32), -1, keepdims=True)
        inv_rms = lax.rsqrt(squares / MODEL_WIDTH + epsilon)
        inv_out[span, :] = jnp.broadcast_to(inv_rms, (height, LANES))
        rows_out[span, :] = (total * inv_rms).astype(bf16)
        if raw is not None:
            raw[span, :] = total


def forward_kernel(group, keep, recv_a, recv_b, seg_col, seg_row, rows_out, inv_out, heads_out):
    make_rows(keep, (recv_a, recv_b), rows_out, inv_out, None)
    kv_heads = heads_out.shape[1] // HEAD_WIDTH // group
    for block in range(keep.shape[0] // BLOCK):
        span = slice(block * BLOCK, (block + 1) * BLOCK)
        for kv_place in range(kv_heads):
            _, _, value, probs = attend(
                rows_out, seg_col, seg_row, span, kv_place, kv_heads, group
            )
            mixed = jnp.dot(probs.astype(bf16), value, preferred_element_type=f32)
            unstack(heads_out, span, kv_place * group, group, mixed.astype(bf16))


def back_blocks(group, rows_ref, seg_col, seg_row, grad_ref, grads_out, heads_out):
    kv_heads = rows_ref.shape[1] // HEAD_WIDTH // (group + 2)
    heads = kv_heads * group
    for block in range(rows_ref.shape[0] // BLOCK):
        span = slice(block * BLOCK, (block + 1) * BLOCK)
        for kv_place in range(kv_heads):
            query, key, value, probs = attend(
                rows_ref, seg_col, seg_row, span, kv_place, kv_heads, group
            )
            rounded = probs.astype(bf16)
            if heads_out is not None:
                mixed = jnp.dot(rounded, value, preferred_element_type=f32)
                unstack(heads_out, span, kv_place * group, group, mixed.astype(bf16))
            grad = stacked(grad_ref, span, kv_place * group, group)
            query_grad, key_grad, value_grad = attend_back(
                query, key, value, probs, rounded, grad
            )
            unstack(grads_out, span, kv_place * group, group, query_grad.astype(bf16))
            unstack(grads_out, span, heads + kv_place, 1, key_grad.astype(bf16))
            unstack(grads_out, span, heads + kv_heads + kv_place, 1, value_grad.astype(bf16))


def sum_grad(keep, recvs, target):
    height = keep.shape[0] // len(recvs)
    for place, recv in enumerate(recvs):
        span = slice(place * height, (place + 1) * height)
        target[span, :] = (keep[span, :] + recv[...].astype(f32)).astype(bf16)


def both_kernel(
    group, keep, recv_a, recv_b, grad_keep, grad_a, grad_b, seg_col, seg_row,
    inv_out, heads_out, grads_out, dots_out, rows, raw, grad,
):
    make_rows(keep, (recv_a, recv_b), rows, inv_out, raw)
    sum_grad(grad_keep, (grad_a, grad_b), grad)
    columns = rows.shape[1]
    back_blocks(group, rows, seg_col, seg_row, grad, grads_out, heads_out)
    dots = jnp.sum(grads_out[:, :columns].astype(f32) * raw[...], -1, keepdims=True)
    dots_out[...] = first_lane(dots)
    grads_out[:, columns:] = high_low(dots)


def back_kernel(group, rows, grad_keep, grad_a, grad_b, seg_col, seg_row, grads_out, grad):
    sum_grad(grad_keep, (grad_a, grad_b), grad)
    back_blocks(group, rows, seg_col, seg_row, grad, grads_out, None)


def out_kernel(heads, wkeep, wsend, keep, send):
    send[...] = jnp.dot(heads[...], wsend[...], preferred_element_type=f32).astype(bf16)
    keep[...] = jnp.dot(heads[...], wkeep[...], preferred_element_type=f32)


def halve_kernel(keep, recv, *outs):
    keeps, sends = outs[: len(outs) // 2], outs[len(outs) // 2 :]
    half = keep.shape[0] // 2
    start = 0
    for out, send in zip(keeps, sends):
        cut = slice(start, start + out.shape[1])
        out[...] = keep[:half, cut] + recv[:half, cut].astype(f32)
        send[...] = (keep[half:, cut] + recv[half:, cut].astype(f32)).astype(bf16)
        start += out.shape[1]


def stream_kernel(start, keep, recv, stream, out):
    quarter = keep.shape[0] // 2
    cut = slice(start, start + out.shape[1])
    for place in range(2):
        span = slice(place * quarter, (place + 1) * quarter)
        back = slice((1 - place) * quarter, (2 - place) * quarter)
        total = keep[span, :] + recv[back, :].astype(f32)
        out[span, :] = (stream[span, cut].astype(f32) + total).astype(bf16)


def grad_kernel(start, keep, recv, grad, stream, inv_ref, dots_ref, out, dots_out):
    quarter = keep.shape[0] // 2
    columns = out.shape[1]
    cut = slice(start, start + columns)
    for place in range(2):
        span = slice(place * quarter, (place + 1) * quarter)
        back = slice((1 - place) * quarter, (2 - place) * quarter)
        total = keep[span, :columns] + recv[back, :columns].astype(f32)
        if dots_out is not None:
            dots = jnp.sum(
                keep[span, columns:] + recv[back, columns:].astype(f32), -1, keepdims=True
            )
            dots_out[span, :] = jnp.broadcast_to(dots, (quarter, LANES))
        else:
            dots = dots_ref[span, 0:1]
        inv_rms = inv_ref[span, 0:1]
        out[span, :] = (
            grad[span, cut].astype(f32)
            + inv_rms * total
            - stream[span, cut].astype(f32) * (inv_rms * inv_rms * inv_rms * dots / MODEL_WIDTH)
        ).astype(bf16)


def grad_first_kernel(keep, recv, grad, stream, inv_ref, out, dots_out):
    grad_kernel(0, keep, recv, grad, stream, inv_ref, None, out, dots_out)


def grad_second_kernel(start, keep, recv, grad, stream, inv_ref, dots_ref, out):
    grad_kernel(start, keep, recv, grad, stream, inv_ref, dots_ref, out, None)


turned = (((1,), (1,)), ((), ()))


def heads_kernel(count, *refs):
    pieces, (wkeep, wsend, keep, send_a, send_b, own_grad, other_grad) = (
        refs[: 2 * count],
        refs[2 * count :],
    )
    assemble(pieces[:count], own_grad)
    assemble(pieces[count:], other_grad)
    keep[...] = lax.dot_general(
        own_grad[...], wkeep[...], turned, preferred_element_type=f32
    ) + lax.dot_general(other_grad[...], wsend[...], turned, preferred_element_type=f32)
    rows = keep.shape[0] // 2
    send_a[...] = keep[:rows, :].astype(bf16)
    send_b[...] = keep[rows:, :].astype(bf16)


def normed_kernel(
    own_grads, other_grads, dots, wkeep, wsend, keep0, keep1, send0, send1, total
):
    inner, columns = wkeep.shape[1], wkeep.shape[0]
    half = keep0.shape[0]
    total[...] = lax.dot_general(
        own_grads[:, :inner], wkeep[...], turned, preferred_element_type=f32
    )
    total[...] += lax.dot_general(
        other_grads[:, :inner], wsend[...], turned, preferred_element_type=f32
    )
    dot_total = jnp.sum(dots[...] + other_grads[:, inner:].astype(f32), -1, keepdims=True)
    middle = columns // 2
    send0[:, :middle] = total[half:, :middle].astype(bf16)
    send0[:, middle:] = high_low(dot_total[half:])
    send1[...] = total[half:, middle:].astype(bf16)
    keep0[:, :middle] = total[:half, :middle]
    keep0[:, middle:] = first_lane(dot_total[:half])
    keep1[...] = total[:half, middle:]


def prelude_kernel(
    place_ref, table, mask, head, grad_out, seg_col, seg_row
):
    core, shard = place_ref[0], place_ref[1]
    micro, slots, packed = table.shape
    packed = packed // 3

    def lengths(m, slot, c):
        return table[m, slot, c]

    def rewards(m, slot, c):
        return table[m, slot, packed + c]

    def groups(m, slot, c):
        return table[m, slot, 2 * packed + c]

    own_slots = slots // 4
    half = grad_out.shape[1]

    def ends(m, slot):
        found, total = [], 0
        for c in range(packed):
            total = total + lengths(m, slot, c)
            found.append(total)
        return found

    def named(m, slot, position):
        name = jnp.full(position.shape, (m * slots + slot) * packed, jnp.int32)
        for end in ends(m, slot):
            name = name + (end <= position).astype(jnp.int32)
        return name

    down = lax.broadcasted_iota(jnp.int32, (SLOT, LANES), 0)
    across = lax.broadcasted_iota(jnp.int32, (8, BLOCK), 1)
    per_block = BLOCK // SLOT
    line = None
    for at in range(4 * micro * own_slots):
        position, m, s = at // (micro * own_slots), at // own_slots % micro, at % own_slots
        slot = (shard ^ (0, 3, 1, 2)[position]) * own_slots + s
        seg_col[at * SLOT : (at + 1) * SLOT, :] = named(m, slot, down)
        inside = at % per_block
        name = named(m, slot, across - inside * SLOT)
        line = name if inside == 0 else jnp.where(across >= inside * SLOT, name, line)
        if inside == per_block - 1:
            first = (at // per_block) * BLOCK
            seg_row[:, first : first + BLOCK] = line

    own_rows = own_slots * SLOT
    for m in range(micro):
        wide = mask[m : m + 1, :].astype(f32)
        turn = lax.broadcasted_iota(jnp.int32, (own_rows, own_rows), 0) == (
            lax.broadcasted_iota(jnp.int32, (own_rows, own_rows), 1)
        )
        masks = jnp.sum(
            jnp.where(turn, jnp.broadcast_to(wide, (own_rows, own_rows)), 0.0), -1, keepdims=True
        )
        for s in range(own_slots):
            slot = shard * own_slots + s
            position = lax.broadcasted_iota(jnp.int32, (SLOT, 1), 0)
            advantage = jnp.zeros((SLOT, 1), f32)
            length = jnp.ones((SLOT, 1), f32)
            before = 0
            for c, end in enumerate(ends(m, slot)):
                mine = groups(m, slot, c)

                def gather(index, carry):
                    total, count, squares = carry
                    other_m = index // (slots * packed)
                    other_s = index // packed % slots
                    other_c = index % packed
                    same = groups(other_m, other_s, other_c) == mine
                    reward = rewards(other_m, other_s, other_c)
                    return (
                        total + jnp.where(same, reward, 0),
                        count + jnp.where(same, 1, 0),
                        squares + jnp.where(same, reward * reward, 0),
                    )

                total, count, squares = lax.fori_loop(
                    0, micro * slots * packed, gather, (jnp.int32(0), jnp.int32(0), jnp.int32(0))
                )

                def column(value):
                    return jnp.full((SLOT, 1), value, jnp.int32).astype(f32)

                centered = column(count * rewards(m, slot, c) - total) / column(count)
                spread = jnp.sqrt(column(count * squares - total * total)) / column(count)
                value = centered / jnp.maximum(spread, 1.0)
                here = (position >= before) & (position < end)
                advantage = jnp.where(here, value, advantage)
                length = jnp.where(here, column(lengths(m, slot, c)), length)
                before = end
            span = slice(s * SLOT, (s + 1) * SLOT)
            weight = -(advantage * SLOT / length * masks[span])
            grad_out[m * own_rows + s * SLOT : m * own_rows + (s + 1) * SLOT, :] = (
                weight * head[m, span, part(core, half)].astype(f32)
            ).astype(bf16)


def turn_kernel(core_ref, one, two, inv_one, inv_two, other, scale_out):
    core = core_ref[0]
    half = one.shape[1]
    first = core == 0
    if inv_one is not None:
        inv = jnp.where(first, inv_one[...], inv_two[...])[:, 0:1]
    for index, value in ((core, None), (1 - core, other[...])):
        if value is None:
            value = jnp.where(first, one[...].astype(f32), two[...].astype(f32))
        value = value.astype(f32)
        if inv_one is not None:
            value = value * inv
        scale_out[part(index, half), :] = value.T.astype(bf16)


def pick_kernel(core_ref, one, two, out):
    @pl.when(core_ref[0] == 0)
    def _():
        out[...] = one[...]

    @pl.when(core_ref[0] != 0)
    def _():
        out[...] = two[...]


def turn_plain_kernel(core_ref, one, two, other, out):
    turn_kernel(core_ref, one, two, None, None, other, out)


def weights_kernel(core_ref, left, *refs):
    rights, outs = refs[:4], refs[4:]
    core = core_ref[0]
    first = core == 0
    start = 0
    for out in outs:
        half = out.shape[1] // 2
        for side in range(2):
            cut = slice(start, start + half)
            right = jnp.where(first, rights[side][:, cut], rights[2 + side][:, cut])
            index = core if side == 0 else 1 - core
            out[:, part(index, half)] = jnp.dot(left[...], right, preferred_element_type=f32)
        start += half


def weight_grads(core_vec, left, rights, widths):
    rows, inner = left.shape
    block = min(512, rows)
    outs = [jax.ShapeDtypeStruct((rows, width), f32) for width in widths]

    def whole(array):
        return pl.BlockSpec(array.shape, lambda i: (0, 0))

    return pl.pallas_call(
        weights_kernel,
        grid=(rows // block,),
        out_shape=outs,
        in_specs=[
            pl.BlockSpec(memory_space=pltpu.SMEM),
            pl.BlockSpec((block, inner), lambda i: (i, 0)),
            *[whole(right) for right in rights],
        ],
        out_specs=[pl.BlockSpec((block, width), lambda i: (i, 0)) for width in widths],
        cost_estimate=pl.CostEstimate(
            flops=2 * rows * inner * sum(widths),
            bytes_accessed=4 * rows * sum(widths),
            transcendentals=0,
        ),
        compiler_params=pltpu.CompilerParams(vmem_limit_bytes=20 << 20),
    )(core_vec, left, *rights)


def spread_tokens(own):
    near, far, cross = (exchange(own, "tp", bit) for bit in (1, 2, 3))
    return [own, cross, near, far]


def local(
    inputs, head_grad, noise_mask, lengths, rewards, groups,
    query_weight, key_weight, value_weight, out_weight,
):
    core = lax.axis_index("pp")
    shard = lax.axis_index("tp")
    micro, own_rows, features = inputs.shape
    half = features // 2
    piece = micro * own_rows
    rows = 4 * piece
    own = [query_weight[0], key_weight[0], value_weight[0], out_weight[0]]
    group = own[0].shape[1] // own[1].shape[1]
    head_cols = own[0].shape[1] // 2
    kv_cols = own[1].shape[1] // 2
    columns = head_cols + 2 * kv_cols
    core_vec = core.astype(jnp.int32)[None]
    place_vec = jnp.stack([core, shard]).astype(jnp.int32)

    def swap(value):
        return exchange(value, "pp", 1)

    def after(value, *others):
        return lax.optimization_barrier((value, *others))[0]

    own_inputs = lax.dynamic_slice_in_dim(inputs, core * half, half, 2).reshape(piece, half)
    pieces = spread_tokens(own_inputs)
    other = [swap(w) for w in own[:3]]
    top_grad, seg_col, seg_row = call(
        prelude_kernel,
        [
            shape(piece, half, bf16),
            shape(rows, LANES, jnp.int32),
            shape(8, rows, jnp.int32),
        ],
        [
            place_vec,
            jnp.concatenate([lengths, rewards, groups], -1),
            noise_mask,
            head_grad,
        ],
        smem=range(2),
    )

    def taken(layer, mine, theirs, height):
        width = sum(w.shape[1] for w in mine) // 2
        return call(
            lambda core_ref, *refs: take(layer, core_ref, len(mine), *refs),
            [shape(height, width, bf16)] * 2,
            [core_vec, *mine, *theirs],
            smem=(0,),
            hbm=range(1, 1 + 2 * len(mine)),
            scratch=[pltpu.SemaphoreType.DMA((2 * len(mine),))],
        )

    in_weights = [taken(0, own[:3], other, half)]
    in_weights.append(taken(1, own[:3], other, half))

    def project(layer, pieces):
        cols = columns + LANES
        keep, send, stream = call(
            functools.partial(project_kernel, len(pieces)),
            [shape(rows, cols, f32), shape(rows, cols, bf16), shape(rows, half, bf16)],
            [*pieces, *in_weights[layer]],
            flops=4 * rows * half * columns,
        )
        return keep, send, stream

    def project_sum(keep, send):
        keep, *sends = add(keep, [swap(send)], 2, True)
        return sum_fsdp(keep, sends, True)

    def head_grads(layer, pieces):
        keep, send_a, send_b, grad, grad_other = call(
            functools.partial(heads_kernel, len(pieces) // 2),
            [
                shape(rows, head_cols, f32),
                *[shape(rows // 2, head_cols, bf16)] * 2,
                *[shape(rows, half, bf16)] * 2,
            ],
            [*pieces, *out_weights[layer]],
            flops=2 * rows * features * head_cols,
        )
        return keep, [send_a, send_b], grad, grad_other

    keep, send, stream0 = project(0, pieces)
    other_out = swap(after(own[3], stream0))
    out_weights = [taken(layer, own[3:], [other_out], head_cols) for layer in (0, 1)]
    top_grad = after(top_grad, stream0)
    top_near = exchange(top_grad, "tp", 1)
    top_far = exchange(jnp.concatenate([top_grad, top_near]), "tp", 3)
    keep, (recv_a, recv_b) = project_sum(keep, send)
    rows0, inv0, heads0 = call(
        functools.partial(forward_kernel, group),
        [shape(rows, columns, bf16), shape(rows, LANES, f32), shape(rows, head_cols, bf16)],
        [keep, recv_a, recv_b, seg_col, seg_row],
        flops=4 * rows * BLOCK * head_cols,
    )

    keep, send = call(
        out_kernel,
        [shape(rows, half, f32), shape(rows, half, bf16)],
        [heads0, *out_weights[0]],
        flops=2 * rows * features * head_cols,
    )
    widths = (half // 2, half // 2)
    *keeps, send0, send1 = call(
        halve_kernel,
        [shape(rows // 2, w, f32) for w in widths] + [shape(rows // 2, w, bf16) for w in widths],
        [keep, swap(send)],
    )
    sends = [send0, send1]

    def cross(bit, sends):
        recvs = []
        for send in sends:
            recvs.append(exchange(send, "tp", bit))
        return recvs

    def add_one(keep, recv, tail):
        return add(keep, [recv], 1, tail)

    def tie(recvs, *others):
        last, *others = lax.optimization_barrier((recvs[1], *others))
        return [recvs[0], last], *others

    recvs = cross(1, sends)
    top_grad, top_near, top_far, _ = lax.optimization_barrier(
        (top_grad, top_near, top_far, (send0, send1))
    )
    (grad1,) = call(
        join_kernel,
        [shape(rows, half, bf16)],
        [top_grad, top_far[:piece], top_near, top_far[piece:]],
    )
    grad1_other = swap(grad1)
    head_keep, head_sends, grad1, grad1_other = head_grads(1, [grad1, grad1_other])
    added = [add_one(keeps[i], recvs[i], False) for i in range(2)]
    recvs = cross(3, [send for _, send in added])
    bits = lax.axis_size("fsdp").bit_length() - 1
    if bits == 2:
        head_recvs = [exchange(value, "fsdp", bit) for value, bit in zip(head_sends, (1, 2))]
        head_keep, *head_sends = add(head_keep, head_recvs, 2, False)
        recvs, head_keep, head_sends = tie(recvs, head_keep, head_sends)
    streams = []
    for place in range(2):
        streams += call(
            functools.partial(stream_kernel, place * widths[0]),
            [shape(rows // 2, widths[place], bf16)],
            [added[place][0], recvs[place], stream0],
        )
    recvs = cross(1, streams)
    if bits == 2:
        head_a, head_b = [exchange(value, "fsdp", bit) for value, bit in zip(head_sends, (2, 1))]
    else:
        head_keep, (head_a, head_b) = sum_fsdp(head_keep, head_sends, False)
    recvs, head_a, head_b = tie(recvs, head_a, head_b)

    keep, send, stream1 = project(1, [*streams, *recvs])
    keep, (recv_a, recv_b) = project_sum(keep, send)
    inv1, heads1, grads1, dots = call(
        functools.partial(both_kernel, group),
        [
            shape(rows, LANES, f32),
            shape(rows, head_cols, bf16),
            shape(rows, columns + LANES, bf16),
            shape(rows, LANES, f32),
        ],
        [keep, recv_a, recv_b, head_keep, head_a, head_b, seg_col, seg_row],
        scratch=[
            pltpu.VMEM((rows, columns), bf16),
            pltpu.VMEM((rows, columns), f32),
            pltpu.VMEM((rows, head_cols), bf16),
        ],
        flops=14 * rows * BLOCK * head_cols,
    )
    grads1_other = swap(grads1)
    *keeps, send0, send1 = call(
        normed_kernel,
        [
            shape(rows // 2, widths[0] + LANES, f32),
            shape(rows // 2, widths[1], f32),
            shape(rows // 2, widths[0] + LANES, bf16),
            shape(rows // 2, widths[1], bf16),
        ],
        [grads1, grads1_other, dots, *in_weights[1]],
        scratch=[pltpu.VMEM((rows, half), f32)],
        flops=4 * rows * half * columns,
    )
    recvs = cross(1, [send0, send1])

    def pick(one, two):
        return call(
            pick_kernel, [shape(*one.shape, one.dtype)], [core_vec, one, two], smem=(0,)
        )[0]

    stream0_late, stream1_late, heads0_late, heads1_late = lax.optimization_barrier(
        (stream0, stream1, heads0, heads1, send1)
    )[:4]
    stream_other = swap(pick(stream1_late, stream0_late))
    (normed,) = call(
        turn_kernel,
        [shape(features, rows, bf16)],
        [core_vec, stream0_late, stream1_late, inv0, inv1, stream_other],
        smem=(0,),
    )
    recvs, normed = tie(recvs, normed)
    added = [add_one(keeps[i], recvs[i], i == 0) for i in range(2)]
    recvs = cross(3, [send for _, send in added])
    heads_other = swap(after(pick(heads1_late, heads0_late), added[1][1]))
    (heads_turned,) = call(
        turn_plain_kernel,
        [shape(2 * head_cols, rows, bf16)],
        [core_vec, heads0_late, heads1_late, heads_other],
        smem=(0,),
    )
    recvs, heads_turned = tie(recvs, heads_turned)
    grad_a, dots = call(
        grad_first_kernel,
        [shape(rows // 2, widths[0], bf16), shape(rows // 2, LANES, f32)],
        [added[0][0], recvs[0], grad1, stream1, inv1],
    )
    (grad_b,) = call(
        functools.partial(grad_second_kernel, widths[0]),
        [shape(rows // 2, widths[1], bf16)],
        [added[1][0], recvs[1], grad1, stream1, inv1, dots],
    )
    recvs = cross(1, [grad_a, grad_b])
    pieces = [grad_a, grad_b, *recvs]

    head_keep, head_sends, grad0, grad0_other = head_grads(
        0, [*pieces, *[swap(value) for value in pieces]]
    )
    (out_weight_grad,) = weight_grads(
        core_vec, heads_turned, [grad0, grad0_other, grad1, grad1_other], [features]
    )
    head_keep, head_recvs = sum_fsdp(head_keep, head_sends, False)
    head_a, head_b, out_weight_grad = lax.optimization_barrier((*head_recvs, out_weight_grad))
    (grads0,) = call(
        functools.partial(back_kernel, group),
        [shape(rows, columns, bf16)],
        [rows0, head_keep, head_a, head_b, seg_col, seg_row],
        scratch=[pltpu.VMEM((rows, head_cols), bf16)],
        flops=12 * rows * BLOCK * head_cols,
    )
    in_grads = weight_grads(
        core_vec,
        normed,
        [grads0, swap(grads0), grads1, grads1_other],
        [2 * head_cols, 2 * kv_cols, 2 * kv_cols],
    )
    return tuple(grad[None] for grad in (*in_grads, out_weight_grad))


def solution(mesh):
    return jax.shard_map(
        local,
        mesh=mesh,
        in_specs=(
            P(None, "tp", "fsdp"),
            P(None, "tp", "fsdp"),
            P(None, "tp"),
            P(),
            P(),
            P(),
            P("pp", "fsdp", "tp"),
            P("pp", "fsdp", "tp"),
            P("pp", "fsdp", "tp"),
            P("pp", "tp", "fsdp"),
        ),
        out_specs=(
            P("pp", "fsdp", "tp"),
            P("pp", "fsdp", "tp"),
            P("pp", "fsdp", "tp"),
            P("pp", "tp", "fsdp"),
        ),
        check_vma=False,
    )
```
